32 devices in a mesh: grp: 2 (over y), row: 4 (over z), mic: 2 (over x), orient: 2 (over core).
Axes of the slice: x: 2, y: 2, z: 4, core: 2. Of those that a mesh axis runs over, the one named last changes fastest.
Arguments:
- spectra: bfloat16 [8, 2, 2048, 2048], P(('grp', 'mic'), None, 'row'), parts along dimension 0, may hold values from -6 to 6
- bank: bfloat16 [8, 384, 384], replicated, as said below
- orient_index: int32 [16], P('grp'), parts along dimension 0, may hold values from 0 to 7, as said below
Outputs:
- peak_map: float32 [8, 4, 512, 128], P(('grp', 'mic'), 'row'), parts along dimension 0
- power_map: float32 [8, 4, 512, 128], P(('grp', 'mic'), 'row'), parts along dimension 0
The draws below stay inside these ranges and needn't reach their ends.
There are 2 independent parts, one for each index of `grp`. The reference program is written for one: setup_inputs(seed, part) draws one part's arguments, and reference() takes and returns one part's arrays. A program takes and returns all parts, laid end to end along the dimension named above; an argument that names none is the same for every part. Nothing has to cross between parts.
Inputs may be any that keep to these rules, and one draw needn't show every extreme that they name: `bank`: projection images of the table. `orient_index`: each entry names one projection of the table; entries may repeat.
All inputs are finite; a program needn't handle non-finite values.
Results may differ from the reference program's by a relative error of at most 0.0051.
Values may be sent and summed in bfloat16 or wider, within the bound.
A program may use at most 128 MiB of HBM per device.

```python
import math
import jax
import jax.numpy as jnp
import numpy as np
from jax import lax

NFFT = 2048
TSIZE = 384
WCOLS = 128
WIN = 8
BANK = 8
MICS = 4
RBANDS = 4
YB = 512


def draw_bank(key, part):
    key_rows = jax.random.fold_in(key, 101)
    key_cols = jax.random.fold_in(key, 202)
    key_noise = jax.random.fold_in(key, 303)
    key_shift = jax.random.fold_in(key, 404)
    row_scale = jnp.exp(jax.random.uniform(key_rows, (BANK, TSIZE, 1), jnp.float32) * math.log(10.0))
    col_scale = jnp.exp(jax.random.uniform(key_cols, (BANK, 1, TSIZE), jnp.float32) * math.log(10.0))
    noise = jax.random.normal(key_noise, (BANK, TSIZE, TSIZE), jnp.float32)
    offset = jax.random.normal(key_shift, (BANK, 1, 1), jnp.float32)
    values = noise * row_scale * col_scale + 3.0 * offset
    return values.astype(jnp.bfloat16)


def draw_orient_index(key, part):
    key_values = jax.random.fold_in(key, 505)
    key_order = jax.random.fold_in(key, 606)
    values = jax.random.randint(key_values, (WIN,), 0, BANK, dtype=jnp.int32)
    order = jax.random.permutation(key_order, WIN)
    positions = jnp.arange(WIN, dtype=jnp.int32)
    values = jnp.where(positions == order[0], BANK - 1, values)
    values = jnp.where(positions == order[1], 0, values)
    return values.astype(jnp.int32)


def block_levels(own_key, shape, pieces, low, top_value):
    level = 1.0
    for dim, shards_of in pieces:
        heights = jax.random.uniform(jax.random.fold_in(jax.random.fold_in(own_key, 6), dim), (shards_of,), jnp.float32, low / len(pieces), top_value / len(pieces))
        level = level * jnp.repeat(jnp.exp(heights), shape[dim] // shards_of).reshape((-1,) + (1,) * (len(shape) - 1 - dim))
    return level


def bell_draw(key, shape, scale, reach, cuts=(), kind=jnp.bfloat16):
    values = jax.random.normal(key, shape, jnp.float32) * scale
    if len(cuts) > 0:
        values = block_levels(key, shape, cuts, -0.22, 0.18) * values
    return jnp.clip(values, min=-reach, max=reach).astype(kind)


def setup_inputs(seed: int = 0, part: int = 0) -> dict:
    keys = jax.random.split(jax.random.key(seed), 4)
    part_keys = jax.random.split(jax.random.fold_in(keys[3], part), 4)
    return {
        "spectra": bell_draw(part_keys[0], (MICS, 2, NFFT, NFFT), 1.0, 6.0, ((0, 2), (2, 4))),
        "bank": draw_bank(jax.random.fold_in(keys[3], 71), part),
        "orient_index": draw_orient_index(jax.random.fold_in(jax.random.fold_in(keys[3], part), 71), part),
    }


two_pi = 2.0 * math.pi

def phase_table(row_start, row_count, col_start, col_count, period):
    row_ids = row_start + jnp.arange(row_count, dtype=jnp.int32)
    col_ids = col_start + jnp.arange(col_count, dtype=jnp.int32)
    wrapped = row_ids[:, None] * col_ids[None, :] % period
    angles = wrapped.astype(jnp.float32) * (two_pi / period)
    return (jnp.cos(angles), jnp.sin(angles))

def normalize(picture):
    values = picture.astype(jnp.float32)
    centred = values - jnp.mean(values)
    factor = lax.rsqrt(jnp.mean(centred * centred) + 1e-06)
    return (centred * factor).astype(jnp.bfloat16)

def reverse_bits(number, digits):
    result = number * 0
    for digit in range(digits):
        result = result + number // (1 << digit) % 2 * (1 << digits - 1 - digit)
    return result

def reference(spectra, bank, orient_index):
    sections = RBANDS.bit_length() - 1
    templates = jax.vmap(normalize)(bank[orient_index])
    cos_y, sin_y = phase_table(0, NFFT, 0, TSIZE, NFFT)
    cos_x, sin_x = phase_table(0, TSIZE, 0, NFFT, NFFT)
    cos_e, sin_e = phase_table(0, NFFT, 0, WCOLS, NFFT)
    cos_y = cos_y.astype(jnp.bfloat16)
    neg_sin_y = -sin_y.astype(jnp.bfloat16)
    cos_x = cos_x.astype(jnp.bfloat16)
    sin_x = sin_x.astype(jnp.bfloat16)
    cos_e = cos_e.astype(jnp.bfloat16)
    sin_e = sin_e.astype(jnp.bfloat16)
    cos_c, sin_c = phase_table(0, NFFT, 0, NFFT, NFFT)
    factor = 1.0 / (NFFT * TSIZE)

    def one_orientation(template):
        pass_re = jnp.dot(cos_y, template, preferred_element_type=jnp.float32).astype(jnp.bfloat16)
        pass_im = jnp.dot(neg_sin_y, template, preferred_element_type=jnp.float32).astype(jnp.bfloat16)
        spec_re = (jnp.dot(pass_re, cos_x, preferred_element_type=jnp.float32) + jnp.dot(pass_im, sin_x, preferred_element_type=jnp.float32)).astype(jnp.bfloat16)
        spec_im = (jnp.dot(pass_im, cos_x, preferred_element_type=jnp.float32) - jnp.dot(pass_re, sin_x, preferred_element_type=jnp.float32)).astype(jnp.bfloat16)
        tmpl_re = spec_re.astype(jnp.float32)
        tmpl_im = spec_im.astype(jnp.float32)

        def one_micrograph(spectrum):
            mic_re = spectrum[0].astype(jnp.float32)
            mic_im = spectrum[1].astype(jnp.float32)
            prod_re = (mic_re * tmpl_re + mic_im * tmpl_im).astype(jnp.bfloat16)
            prod_im = (mic_im * tmpl_re - mic_re * tmpl_im).astype(jnp.bfloat16)
            part_re = jnp.dot(prod_re, cos_e, preferred_element_type=jnp.float32) - jnp.dot(prod_im, sin_e, preferred_element_type=jnp.float32)
            part_im = jnp.dot(prod_re, sin_e, preferred_element_type=jnp.float32) + jnp.dot(prod_im, cos_e, preferred_element_type=jnp.float32)
            column = jnp.dot(cos_c, part_re, precision=lax.Precision.HIGHEST) - jnp.dot(sin_c, part_im, precision=lax.Precision.HIGHEST)
            return column * factor
        return lax.map(one_micrograph, spectra)

    def accumulate(carry, template):
        corr = one_orientation(template)
        return ((jnp.maximum(carry[0], corr), carry[1] + corr * corr), None)
    start_peak = jnp.full((MICS, NFFT, WCOLS), -1e+30, jnp.float32)
    start_power = jnp.zeros((MICS, NFFT, WCOLS), jnp.float32)
    totals, unused = lax.scan(accumulate, (start_peak, start_power), templates)
    reversal = np.array([reverse_bits(place, sections) for place in range(RBANDS)], dtype=np.int32)

    def arrange(field):
        shaped = field.reshape(MICS, YB, RBANDS, WCOLS).transpose(0, 2, 1, 3)
        return shaped[:, reversal]
    return (arrange(totals[0]), arrange(totals[1]))
```

```python
import functools
import math

import jax
import jax.numpy as jnp
import numpy as np
from jax import lax
from jax.experimental import pallas as pl
from jax.experimental.pallas import tpu as pltpu
from jax.sharding import PartitionSpec as P

WCOLS = 128
MESH = pl.DeviceIdType.MESH
EXTRA = 16
MAPS = jnp.bfloat16
PARTS = 4


two_pi = 2.0 * math.pi


def swapped(shard, axis, apart):
    return lax.ppermute(shard, axis, [(i, i ^ 1 << apart) for i in range(lax.axis_size(axis))])


def merged_2(part, axis, combine):
    gathered = jax.tree.map(lambda a: lax.all_gather(a, axis), part)

    def take(source):
        return jax.tree.map(lambda a: lax.dynamic_index_in_dim(a, source, 0, False), gathered)

    return lax.fori_loop(
        1, lax.axis_size(axis), lambda source, state: combine(state, take(source)), take(0)
    )


def phase_table(row_start, row_count, col_start, col_count, period):
    row_ids = row_start + jnp.arange(row_count, dtype=jnp.int32)
    col_ids = col_start + jnp.arange(col_count, dtype=jnp.int32)
    wrapped = row_ids[:, None] * col_ids[None, :] % period
    angles = wrapped.astype(jnp.float32) * (two_pi / period)
    return (jnp.cos(angles), jnp.sin(angles))


def normalize(picture):
    values = picture.astype(jnp.float32)
    centred = values - jnp.mean(values)
    factor = lax.rsqrt(jnp.mean(centred * centred) + 1e-06)
    return (centred * factor).astype(jnp.bfloat16)


def reverse_bits(number, digits):
    result = number * 0
    for digit in range(digits):
        result = result + number // (1 << digit) % 2 * (1 << digits - 1 - digit)
    return result


def combine_maps(first_pair, second_pair):
    return (jnp.maximum(first_pair[0], second_pair[0]), first_pair[1] + second_pair[1])


def shards_general(spectra, bank, orient_index):
    mic_count = spectra.shape[0]
    band_rows = spectra.shape[2]
    length = spectra.shape[3]
    tsize_px = bank.shape[1]
    row_devices = lax.axis_size("row")
    row_place = lax.axis_index("row")
    share_count = orient_index.shape[0] // lax.axis_size("orient")
    chosen = lax.dynamic_slice_in_dim(
        orient_index, lax.axis_index("orient") * share_count, share_count
    )
    templates = jnp.stack(
        [
            normalize(lax.dynamic_index_in_dim(bank, chosen[place], 0, False))
            for place in range(share_count)
        ]
    )
    cos_y, sin_y = phase_table(row_place * band_rows, band_rows, 0, tsize_px, length)
    left_table = jnp.concatenate([cos_y.astype(jnp.bfloat16), -sin_y.astype(jnp.bfloat16)], 0)
    rowpass = jnp.einsum(
        "ay,oyx->oax", left_table, templates, preferred_element_type=jnp.float32
    ).astype(jnp.bfloat16)
    cos_x, sin_x = phase_table(0, tsize_px, 0, length, length)
    right_table = jnp.concatenate([cos_x.astype(jnp.bfloat16), sin_x.astype(jnp.bfloat16)], 1)
    mixed = jnp.einsum("oax,xk->oak", rowpass, right_table, preferred_element_type=jnp.float32)
    upper_rows = mixed[:, :band_rows]
    lower_rows = mixed[:, band_rows:]
    spec_re = upper_rows[:, :, :length] + lower_rows[:, :, length:]
    spec_im = lower_rows[:, :, :length] - upper_rows[:, :, length:]
    piece = jnp.stack([spec_re, spec_im], 1).astype(jnp.bfloat16)
    cos_e, sin_e = phase_table(0, length, 0, WCOLS, length)
    row_table = jnp.concatenate([cos_e.astype(jnp.bfloat16), sin_e.astype(jnp.bfloat16)], 1)
    updates = []
    for orient_pos in range(share_count):
        tmpl_re = piece[orient_pos, 0].astype(jnp.float32)
        tmpl_im = piece[orient_pos, 1].astype(jnp.float32)
        mic_re = spectra[:, 0].astype(jnp.float32)
        mic_im = spectra[:, 1].astype(jnp.float32)
        prod_re = mic_re * tmpl_re + mic_im * tmpl_im
        prod_im = mic_im * tmpl_re - mic_re * tmpl_im
        product = jnp.stack([prod_re, prod_im], 1).astype(jnp.bfloat16)
        summed = jnp.einsum("mcbk,kw->mcbw", product, row_table, preferred_element_type=jnp.float32)
        part_re = summed[:, 0, :, :WCOLS] - summed[:, 1, :, WCOLS:]
        part_im = summed[:, 0, :, WCOLS:] + summed[:, 1, :, :WCOLS]
        updates.append(jnp.stack([part_re, part_im], 1))
    partial_value = jnp.stack(updates, 1)
    item_total = mic_count * share_count
    values = partial_value.reshape(item_total, 2, band_rows, WCOLS)
    sections = row_devices.bit_length() - 1
    for bit in reversed(range(sections)):
        half_span = 1 << bit
        partner = swapped(values, "row", bit)
        upper_side = row_place // half_span % 2
        offset = row_place % half_span
        twist = offset.astype(jnp.float32) * (math.pi / half_span)
        twist_re = jnp.cos(twist)
        twist_im = jnp.sin(twist)
        differ = partner - values
        rot_re = differ[:, 0] * twist_re - differ[:, 1] * twist_im
        rot_im = differ[:, 0] * twist_im + differ[:, 1] * twist_re
        rotated = jnp.stack([rot_re, rot_im], 1)
        values = jnp.where(upper_side == 1, rotated, values + partner)
    residue = reverse_bits(row_place, sections)
    pixel_rows = residue + row_devices * jnp.arange(band_rows, dtype=jnp.int32)
    local_rows = jnp.arange(band_rows, dtype=jnp.int32)
    wrapped_col = pixel_rows[:, None] * local_rows[None, :] % length
    col_angles = wrapped_col.astype(jnp.float32) * (two_pi / length)
    column_table = jnp.stack([jnp.cos(col_angles), -jnp.sin(col_angles)], 1)
    corr = jnp.einsum("tcj,icjw->itw", column_table, values, precision=lax.Precision.HIGHEST)
    corr = corr * (1.0 / (length * tsize_px))
    corr = corr.reshape(mic_count, share_count, band_rows, WCOLS)
    peak_part = jnp.max(corr, axis=1)
    power_part = jnp.sum(corr * corr, axis=1)
    merged = merged_2((peak_part, power_part), "orient", combine_maps)
    return (merged[0][:, None], merged[1][:, None])


def rotation(rows, cols, period):
    angle = np.outer(rows, cols) % period * (two_pi / period)
    return np.cos(angle), np.sin(angle)


def fused_kernel(
    sizes,
    index_ref, spectra_ref, bank_ref,
    enter_hbm, left_hbm, wide_hbm, short_hbm, leave_hbm, col_hi_hbm, col_lo_hbm, twc_hbm, tws_hbm,
    final,
    spec, bank, enter, left, wide, short, leave, col_hi, col_lo, twc, tws,
    own_s, send_s, recv_s, folded, rowpass, tspec, window, prod, p_send, p_all,
    v_hi, v_lo, corr_acc,
    own, sibling, merged,
    spec_sem, load_sem, fold_send, fold_recv, share_send, share_recv, send_sem, recv_sem,
    pair_send, pair_recv, map_send, map_recv, fwd_send, fwd_recv,
):
    bands, share, band, length, tsize = sizes
    half = WCOLS // 2
    hb = band // 2
    pb = band // PARTS
    full = band + EXTRA
    win = tsize + WCOLS
    me = lax.axis_index("row")
    core = lax.axis_index("orient")
    side = me // 2
    mirror = bands - 1 - me
    level = me + side * (mirror - me)
    peer = me + 1 - 2 * (me % 2)

    def spec_load(mic, k):
        block = k + side * (PARTS - 1 - 2 * k)
        rows = pl.ds(pl.multiple_of(block * pb, pb), pb)
        slot = mic * PARTS + k
        which = (1 - side) if mic == 0 else side
        return pltpu.make_async_copy(
            spectra_ref.at[which, :, rows, :], spec.at[slot], spec_sem.at[slot]
        )

    first_rows = pl.ds(pl.multiple_of(level * band, band), full)
    loads = [
        pltpu.make_async_copy(source, target, load_sem.at[n])
        for n, (source, target) in enumerate(
            [
                (enter_hbm.at[core], enter),
                (bank_ref, bank),
                (left_hbm.at[:, first_rows, :], left),
                (short_hbm, short),
                (wide_hbm, wide),
                (leave_hbm.at[me % 2], leave),
                (col_hi_hbm, col_hi),
                (col_lo_hbm, col_lo),
                (twc_hbm, twc),
                (tws_hbm, tws),
            ]
        )
    ]
    spec_load(0, 0).start()
    loads[0].start()
    for k in range(1, PARTS):
        spec_load(0, k).start()
    for k in range(PARTS):
        spec_load(1, k).start()
    for load in loads[1:]:
        load.start()
    barrier = pltpu.get_barrier_semaphore()
    for k in range(1, bands):
        pl.semaphore_signal(
            barrier, inc=1, device_id={"row": lax.rem(me + k, bands)}, device_id_type=MESH
        )
    pl.semaphore_signal(barrier, inc=1, device_id={"orient": 1 - core}, device_id_type=MESH)

    row_i = lax.broadcasted_iota(jnp.int32, (pb, pb), 0)
    col_i = lax.broadcasted_iota(jnp.int32, (pb, pb), 1)
    target = row_i + side * ((pb - row_i) % pb - row_i)
    turn = jnp.where(col_i == target, 1.0, 0.0).astype(jnp.bfloat16)
    lane = lax.broadcasted_iota(jnp.int32, (1, win), 1)
    sign = jnp.where(lane < win // 2, 1.0, 1.0 - 2.0 * side.astype(jnp.float32))
    parity = (1 - 2 * core).astype(jnp.bfloat16)

    def chunk_rows(k):
        return pl.ds(k * pb, pb + (EXTRA if k == PARTS - 1 else 0))

    def fold_copy(k):
        rows = chunk_rows(k)
        return pltpu.make_async_remote_copy(
            src_ref=send_s.at[rows, :], dst_ref=recv_s.at[rows, :],
            send_sem=fold_send.at[k], recv_sem=fold_recv.at[k],
            device_id={"row": mirror}, device_id_type=MESH,
        )

    def enter_window(mic, target_ref, after):
        carry = jnp.zeros((1, win), jnp.float32)
        for k in range(PARTS):
            spec_load(mic, k).wait()
            if mic == 0 and k == 0:
                loads[0].wait()
            slot = mic * PARTS + k
            total = None
            for part in range(2):
                low = spec[slot, part, :, pl.ds(0, length // 2)]
                high = spec[slot, part, :, pl.ds(length // 2, length // 2)]
                mixed = low + high * parity
                value = jnp.dot(
                    mixed, enter[pl.ds(part * (length // 2), length // 2), :],
                    preferred_element_type=jnp.float32,
                )
                total = value if total is None else total + value
            total = (total * sign).astype(jnp.bfloat16)
            turned = jnp.dot(turn, total, preferred_element_type=jnp.float32)
            rowid = lax.broadcasted_iota(jnp.int32, (pb, win), 0)
            placed = jnp.where(rowid == side - 1, carry, turned)
            carry = turned[0:1, :]
            target_ref[pl.ds(k * pb, pb), :] = placed.astype(jnp.bfloat16)
            if k == PARTS - 1:
                rowid = lax.broadcasted_iota(jnp.int32, (EXTRA, win), 0)
                last = jnp.where(rowid == side - 1, carry, 0.0)
                target_ref[pl.ds(band, EXTRA), :] = last.astype(jnp.bfloat16)
            after(k)

    def send_chunk(k):
        if k == 0:
            pl.semaphore_wait(barrier, bands)
        fold_copy(k).start()

    enter_window(0, send_s, send_chunk)
    enter_window(1, own_s, lambda k: None)

    for n in range(1, 4):
        loads[n].wait()
    step = full // 3

    def template_body(o, carry):
        picture = bank[index_ref[core * share + o]].astype(jnp.float32)
        centred = picture - jnp.mean(picture)
        scale = lax.rsqrt(jnp.mean(centred * centred) + 1e-06)
        template = (centred * scale).astype(jnp.bfloat16)
        for block in range(3):
            rows = pl.ds(block * step, step)
            for part in range(2):
                value = jnp.dot(left[part, rows, :], template, preferred_element_type=jnp.float32)
                rowpass[rows, pl.ds(part * tsize, tsize)] = value.astype(jnp.bfloat16)
        for block in range(3):
            rows = pl.ds(block * step, step)
            tspec[o, rows, :] = jnp.dot(
                rowpass[rows, :], short[...], preferred_element_type=jnp.float32
            )
        return carry

    lax.fori_loop(0, share, template_body, 0)
    for n in range(4, 10):
        loads[n].wait()

    def share_copy(k, source):
        rows = chunk_rows(k)
        return pltpu.make_async_remote_copy(
            src_ref=folded.at[source, rows, :], dst_ref=folded.at[source, rows, :],
            send_sem=share_send.at[k], recv_sem=share_recv.at[k],
            device_id={"orient": 1 - core}, device_id_type=MESH,
        )

    def part_copy(source, o, k):
        rows = chunk_rows(k)
        return pltpu.make_async_remote_copy(
            src_ref=p_send.at[o, rows, :], dst_ref=p_all.at[source, o, rows, :],
            send_sem=send_sem.at[o, k], recv_sem=recv_sem.at[o, k],
            device_id={"row": peer}, device_id_type=MESH,
        )

    def product_chunk(k):
        rows = chunk_rows(k)
        count = pb + (EXTRA if k == PARTS - 1 else 0)
        fold_copy(k).wait_recv()
        total = own_s[rows, :].astype(jnp.float32) + recv_s[rows, :].astype(jnp.float32)
        folded[core, rows, :] = total.astype(jnp.bfloat16)
        share_copy(k, core).start()
        value = jnp.dot(folded[core, rows, :], wide[core], preferred_element_type=jnp.float32)
        window[pl.ds(0, count), :] = value
        share_copy(k, 1 - core).wait_recv()
        value = jnp.dot(folded[1 - core, rows, :], wide[1 - core], preferred_element_type=jnp.float32)
        window[pl.ds(0, count), :] += value

        def orient_body(o, carry):
            m_re = window[pl.ds(0, count), pl.ds(0, win)]
            m_im = window[pl.ds(0, count), pl.ds(win, win)]
            t_re = tspec[o, rows, pl.ds(0, win)]
            t_im = tspec[o, rows, pl.ds(win, win)]
            prod[pl.ds(0, count), pl.ds(0, win)] = (m_re * t_re + m_im * t_im).astype(jnp.bfloat16)
            prod[pl.ds(0, count), pl.ds(win, win)] = (m_im * t_re - m_re * t_im).astype(jnp.bfloat16)
            value = jnp.dot(prod[pl.ds(0, count), :], leave[...], preferred_element_type=jnp.float32)
            value = value.astype(jnp.bfloat16)
            p_all[level, o, rows, :] = value[:, :WCOLS]
            p_send[o, rows, :] = value[:, WCOLS:]
            part_copy(level, o, k).start()
            return carry

        lax.fori_loop(0, share, orient_body, 0)

    rc = 64
    factor = 1.0 / (length * tsize * win)

    def column_chunk(k):
        def orient_body(o, carry):
            part_copy(1 - level, o, k).wait_recv()
            for c in range(pb // rc):
                rows = pl.ds(k * pb + c * rc, rc)
                first = lax.broadcasted_iota(jnp.int32, (rc, WCOLS), 1) < half
                b0, b1 = [p_all[b, o, rows, :].astype(jnp.float32) for b in range(2)]
                turned = pltpu.roll(b1, half, 1)
                turned = jnp.where(first, -turned, turned)
                u = [b0 + b1, b0 + turned, b0 - b1, b0 - turned]
                v = [u[0]]
                for rho in range(1, 4):
                    span = pl.ds((rho - 1) * WCOLS, WCOLS)
                    v.append(
                        u[rho] * twc[rows, span] + pltpu.roll(u[rho], half, 1) * tws[rows, span]
                    )
                for pair in range(2):
                    even, odd = v[2 * pair], v[2 * pair + 1]
                    v_re = jnp.where(first, even, pltpu.roll(odd, half, 1))
                    v_im = jnp.where(first, pltpu.roll(even, half, 1), odd)
                    span = pl.ds(pair * WCOLS, WCOLS)
                    for part, value in enumerate((v_re, v_im)):
                        high = value.astype(jnp.bfloat16)
                        where = pl.ds(part * pb + c * rc, rc)
                        v_hi[where, span] = high
                        v_lo[where, span] = (value - high.astype(jnp.float32)).astype(jnp.bfloat16)
            cols = pl.ds(k * 2 * pb, 2 * pb)
            high, low = col_hi[:, cols], col_lo[:, cols]
            corr = jnp.dot(high, v_hi[...], preferred_element_type=jnp.float32)
            corr += jnp.dot(low, v_hi[...], preferred_element_type=jnp.float32)
            corr += jnp.dot(high, v_lo[...], preferred_element_type=jnp.float32)
            if k == 0:
                corr_acc[o] = corr
            else:
                corr_acc[o] += corr
            return carry

        lax.fori_loop(0, share, orient_body, 0)

    for k in range(PARTS):
        product_chunk(k)
        if k > 0:
            column_chunk(k - 1)
    column_chunk(PARTS - 1)

    edge = []
    for o in range(share):
        e0, e1 = [p_all[b, o, pl.ds(band, EXTRA), :].astype(jnp.float32) for b in range(2)]
        first = lax.broadcasted_iota(jnp.int32, (EXTRA, WCOLS), 1) < half
        swapped_0, swapped_1 = pltpu.roll(e0, half, 1), pltpu.roll(e1, half, 1)
        edge.append(
            [
                jnp.where(first, e0 + e1, -e0 - swapped_1)[0:1, :],
                jnp.where(first, e1 - e0, e0 - swapped_1)[0:1, :],
            ]
        )

    first = lax.broadcasted_iota(jnp.int32, (band, WCOLS), 1) < half
    for pair in range(2):
        span = pl.ds(pair * WCOLS, WCOLS)
        hi = po = None
        for o in range(share):
            corr = (corr_acc[o, :, span] + edge[o][pair]) * factor
            hi = corr if o == 0 else jnp.maximum(hi, corr)
            po = corr * corr if o == 0 else po + corr * corr
        own[pair] = jnp.where(first, hi, pltpu.roll(po, half, 1))
        own[pair + 2] = jnp.where(first, pltpu.roll(hi, half, 1), po)

    mine = pl.ds(pl.multiple_of(core * hb, hb), hb)
    theirs = pl.ds(pl.multiple_of((1 - core) * hb, hb), hb)

    def swap(k):
        q = lax.rem(me + k, bands)
        return pltpu.make_async_remote_copy(
            src_ref=own.at[q, theirs, :], dst_ref=sibling.at[q],
            send_sem=pair_send.at[k], recv_sem=pair_recv.at[k],
            device_id={"orient": 1 - core}, device_id_type=MESH,
        )

    for k in (2, 1, 3, 0):
        swap(k).start()
    first = lax.broadcasted_iota(jnp.int32, (hb, WCOLS), 1) < half

    def map_copy(k, source):
        dest = lax.rem(me + k, bands)
        return pltpu.make_async_remote_copy(
            src_ref=merged.at[dest], dst_ref=final.at[source, mine, :],
            send_sem=map_send.at[k], recv_sem=map_recv.at[source],
            device_id={"row": dest}, device_id_type=MESH,
        )

    def forward(source, rows):
        return pltpu.make_async_remote_copy(
            src_ref=final.at[source, rows, :], dst_ref=final.at[source, rows, :],
            send_sem=fwd_send.at[source], recv_sem=fwd_recv.at[source],
            device_id={"orient": 1 - core}, device_id_type=MESH,
        )

    for k in (2, 1, 3, 0):
        swap(k).wait_recv()
        q = lax.rem(me + k, bands)
        one, two = own[q, mine, :], sibling[q]
        total = jnp.where(first, jnp.maximum(one, two), one + two).astype(final.dtype)
        if k == 0:
            final[me, mine, :] = total
        else:
            merged[q] = total
            map_copy(k, me).start()
    forward(me, mine).start()
    for k in (1, 3, 2):
        source = lax.rem(me + k, bands)
        map_copy(k, source).wait_recv()
        forward(source, mine).start()
    for source in range(4):
        forward(source, theirs).wait_recv()
    for source in range(4):
        forward(source, mine).wait_send()
    for k in range(1, bands):
        map_copy(k, me).wait_send()
    for k in range(bands):
        swap(k).wait_send()
    for k in range(PARTS):
        fold_copy(k).wait_send()
        share_copy(k, core).wait_send()
        for o in range(share):
            part_copy(level, o, k).wait_send()


def assemble_kernel(maps, peak_ref, power_ref):
    half = WCOLS // 2
    first = lax.broadcasted_iota(jnp.int32, maps.shape[1:], 1) < half
    a, b = maps[0].astype(jnp.float32), maps[1].astype(jnp.float32)
    peak_ref[0, 0] = jnp.where(first, a, pltpu.roll(b, half, 1))
    power_ref[0, 0] = jnp.where(first, pltpu.roll(a, half, 1), b)


def shards_fused(spectra, bank, orient_index):
    band = spectra.shape[2]
    length = spectra.shape[3]
    tsize = bank.shape[1]
    bands = lax.axis_size("row")
    share = orient_index.shape[0] // lax.axis_size("orient")
    half = WCOLS // 2
    win = tsize + WCOLS
    pb = band // PARTS
    full = band + EXTRA
    bf, f32 = jnp.bfloat16, jnp.float32

    def low(table):
        return np.ascontiguousarray(table).astype(np.float32).astype(bf)

    def blocks(re, im):
        return np.concatenate([np.concatenate([re, im], 1), np.concatenate([-im, re], 1)], 0)

    kx = np.arange(length // 2)
    place = np.arange(win // 2)
    enter = np.stack([blocks(*rotation(kx, 2 * place + c, length)) for c in range(2)])
    ky = np.arange(2 * band + EXTRA)
    cos_y, sin_y = rotation(ky, np.arange(tsize), length)
    left = np.stack([cos_y, -sin_y])
    freq = np.arange(win)

    def forward_table(points):
        cosine, sine = rotation(points, freq, win)
        return blocks(cosine, -sine)

    wide = np.stack([forward_table(2 * place + c) for c in range(2)])
    short = forward_table(np.arange(tsize))
    leave = []
    for xh in range(2):
        tiles = []
        for h in (xh, 1 - xh):
            tiles.append(blocks(*rotation(freq, h * half + np.arange(half), win)))
        leave.append(np.concatenate(tiles, 1))
    leave = np.stack(leave)
    at = np.arange(2 * band)
    col_j = at // (2 * pb) * pb + at % pb
    cos_c, sin_c = rotation(np.arange(band), col_j, band)
    column = np.where(at // pb % 2 == 0, cos_c, -sin_c).astype(np.float32)
    col_hi = low(column)
    col_lo = low(column - col_hi.astype(np.float32))
    rho = np.repeat(np.arange(1, 4), WCOLS)
    twc, tws = rotation(np.arange(band), rho, length)
    tws = np.where(np.arange(3 * WCOLS) % WCOLS < half, -tws, tws)
    tables = [
        low(enter), low(left), low(wide), low(short), low(leave), col_hi, col_lo,
        twc.astype(np.float32), tws.astype(np.float32),
    ]
    vmem = pl.BlockSpec(memory_space=pltpu.VMEM)
    hbm = pl.BlockSpec(memory_space=pl.ANY)
    dma = pltpu.SemaphoreType.DMA
    maps = pl.pallas_call(
        functools.partial(fused_kernel, (bands, share, band, length, tsize)),
        out_shape=jax.ShapeDtypeStruct((4, band, WCOLS), MAPS),
        in_specs=[pl.BlockSpec(memory_space=pltpu.SMEM)] + [hbm] * (2 + len(tables)),
        out_specs=vmem,
        scratch_shapes=[
            pltpu.VMEM((2 * PARTS, 2, pb, length), bf),
            pltpu.VMEM(bank.shape, bf),
            pltpu.VMEM((length, win), bf),
            pltpu.VMEM((2, full, tsize), bf),
            pltpu.VMEM((2, win, 2 * win), bf),
            pltpu.VMEM((2 * tsize, 2 * win), bf),
            pltpu.VMEM((2 * win, 2 * WCOLS), bf),
            pltpu.VMEM((band, 2 * band), bf),
            pltpu.VMEM((band, 2 * band), bf),
            pltpu.VMEM((band, 3 * WCOLS), f32),
            pltpu.VMEM((band, 3 * WCOLS), f32),
            pltpu.VMEM((full, win), bf),
            pltpu.VMEM((full, win), bf),
            pltpu.VMEM((full, win), bf),
            pltpu.VMEM((2, full, win), bf),
            pltpu.VMEM((full, 2 * tsize), bf),
            pltpu.VMEM((share, full, 2 * win), f32),
            pltpu.VMEM((pb + EXTRA, 2 * win), f32),
            pltpu.VMEM((pb + EXTRA, 2 * win), bf),
            pltpu.VMEM((share, full, WCOLS), bf),
            pltpu.VMEM((2, share, full, WCOLS), bf),
            pltpu.VMEM((2 * pb, 2 * WCOLS), bf),
            pltpu.VMEM((2 * pb, 2 * WCOLS), bf),
            pltpu.VMEM((share, band, 2 * WCOLS), f32),
            pltpu.VMEM((4, band, WCOLS), f32),
            pltpu.VMEM((4, band // 2, WCOLS), f32),
            pltpu.VMEM((4, band // 2, WCOLS), MAPS),
            dma((2 * PARTS,)),
            dma((10,)),
            dma((PARTS,)),
            dma((PARTS,)),
            dma((PARTS,)),
            dma((PARTS,)),
            dma((share, PARTS)),
            dma((share, PARTS)),
            dma((bands,)),
            dma((bands,)),
            dma((bands,)),
            dma((bands,)),
            dma((bands,)),
            dma((bands,)),
        ],
        compiler_params=pltpu.CompilerParams(
            collective_id=0, has_side_effects=True, vmem_limit_bytes=58 << 20
        ),
    )(orient_index, spectra, bank, *tables)
    out = jax.ShapeDtypeStruct((2, 1, band, WCOLS), f32)
    one_mic = pl.BlockSpec((1, 1, band, WCOLS), lambda m: (m, 0, 0, 0))
    return pl.pallas_call(
        assemble_kernel,
        grid=(2,),
        out_shape=(out, out),
        in_specs=[pl.BlockSpec((2, band, WCOLS), lambda m: (m, 0, 0))],
        out_specs=(one_mic, one_mic),
    )(maps)


def shards(spectra, bank, orient_index):
    fits = (
        lax.axis_size("row") == 4
        and lax.axis_size("orient") == 2
        and spectra.shape[0] == 2
        and spectra.shape[2] == 4 * WCOLS
        and bank.shape[1] == 3 * WCOLS
        and spectra.shape[3] == 4 * spectra.shape[2]
    )
    body = shards_fused if fits else shards_general
    return body(spectra, bank, orient_index)


def solution(mesh):
    return jax.shard_map(
        shards,
        mesh=mesh,
        in_specs=(P(("grp", "mic"), None, "row", None), P(), P("grp")),
        out_specs=(P(("grp", "mic"), "row", None, None), P(("grp", "mic"), "row", None, None)),
        check_vma=False,
    )
```

```python
import functools
import math

import jax
import jax.numpy as jnp
import numpy as np
from jax import lax
from jax.experimental import pallas as pl
from jax.experimental.pallas import tpu as pltpu
from jax.sharding import PartitionSpec as P

WCOLS = 128
MESH = pl.DeviceIdType.MESH
EXTRA = 16
MAPS = jnp.bfloat16
CHUNKS = (128, 128, 128, 64, 64)


two_pi = 2.0 * math.pi


def swapped(shard, axis, apart):
    return lax.ppermute(shard, axis, [(i, i ^ 1 << apart) for i in range(lax.axis_size(axis))])


def merged_2(part, axis, combine):
    gathered = jax.tree.map(lambda a: lax.all_gather(a, axis), part)

    def take(source):
        return jax.tree.map(lambda a: lax.dynamic_index_in_dim(a, source, 0, False), gathered)

    return lax.fori_loop(
        1, lax.axis_size(axis), lambda source, state: combine(state, take(source)), take(0)
    )


def phase_table(row_start, row_count, col_start, col_count, period):
    row_ids = row_start + jnp.arange(row_count, dtype=jnp.int32)
    col_ids = col_start + jnp.arange(col_count, dtype=jnp.int32)
    wrapped = row_ids[:, None] * col_ids[None, :] % period
    angles = wrapped.astype(jnp.float32) * (two_pi / period)
    return (jnp.cos(angles), jnp.sin(angles))


def normalize(picture):
    values = picture.astype(jnp.float32)
    centred = values - jnp.mean(values)
    factor = lax.rsqrt(jnp.mean(centred * centred) + 1e-06)
    return (centred * factor).astype(jnp.bfloat16)


def reverse_bits(number, digits):
    result = number * 0
    for digit in range(digits):
        result = result + number // (1 << digit) % 2 * (1 << digits - 1 - digit)
    return result


def combine_maps(first_pair, second_pair):
    return (jnp.maximum(first_pair[0], second_pair[0]), first_pair[1] + second_pair[1])


def shards_general(spectra, bank, orient_index):
    mic_count = spectra.shape[0]
    band_rows = spectra.shape[2]
    length = spectra.shape[3]
    tsize_px = bank.shape[1]
    row_devices = lax.axis_size("row")
    row_place = lax.axis_index("row")
    share_count = orient_index.shape[0] // lax.axis_size("orient")
    chosen = lax.dynamic_slice_in_dim(
        orient_index, lax.axis_index("orient") * share_count, share_count
    )
    templates = jnp.stack(
        [
            normalize(lax.dynamic_index_in_dim(bank, chosen[place], 0, False))
            for place in range(share_count)
        ]
    )
    cos_y, sin_y = phase_table(row_place * band_rows, band_rows, 0, tsize_px, length)
    left_table = jnp.concatenate([cos_y.astype(jnp.bfloat16), -sin_y.astype(jnp.bfloat16)], 0)
    rowpass = jnp.einsum(
        "ay,oyx->oax", left_table, templates, preferred_element_type=jnp.float32
    ).astype(jnp.bfloat16)
    cos_x, sin_x = phase_table(0, tsize_px, 0, length, length)
    right_table = jnp.concatenate([cos_x.astype(jnp.bfloat16), sin_x.astype(jnp.bfloat16)], 1)
    mixed = jnp.einsum("oax,xk->oak", rowpass, right_table, preferred_element_type=jnp.float32)
    upper_rows = mixed[:, :band_rows]
    lower_rows = mixed[:, band_rows:]
    spec_re = upper_rows[:, :, :length] + lower_rows[:, :, length:]
    spec_im = lower_rows[:, :, :length] - upper_rows[:, :, length:]
    piece = jnp.stack([spec_re, spec_im], 1).astype(jnp.bfloat16)
    cos_e, sin_e = phase_table(0, length, 0, WCOLS, length)
    row_table = jnp.concatenate([cos_e.astype(jnp.bfloat16), sin_e.astype(jnp.bfloat16)], 1)
    updates = []
    for orient_pos in range(share_count):
        tmpl_re = piece[orient_pos, 0].astype(jnp.float32)
        tmpl_im = piece[orient_pos, 1].astype(jnp.float32)
        mic_re = spectra[:, 0].astype(jnp.float32)
        mic_im = spectra[:, 1].astype(jnp.float32)
        prod_re = mic_re * tmpl_re + mic_im * tmpl_im
        prod_im = mic_im * tmpl_re - mic_re * tmpl_im
        product = jnp.stack([prod_re, prod_im], 1).astype(jnp.bfloat16)
        summed = jnp.einsum("mcbk,kw->mcbw", product, row_table, preferred_element_type=jnp.float32)
        part_re = summed[:, 0, :, :WCOLS] - summed[:, 1, :, WCOLS:]
        part_im = summed[:, 0, :, WCOLS:] + summed[:, 1, :, :WCOLS]
        updates.append(jnp.stack([part_re, part_im], 1))
    partial_value = jnp.stack(updates, 1)
    item_total = mic_count * share_count
    values = partial_value.reshape(item_total, 2, band_rows, WCOLS)
    sections = row_devices.bit_length() - 1
    for bit in reversed(range(sections)):
        half_span = 1 << bit
        partner = swapped(values, "row", bit)
        upper_side = row_place // half_span % 2
        offset = row_place % half_span
        twist = offset.astype(jnp.float32) * (math.pi / half_span)
        twist_re = jnp.cos(twist)
        twist_im = jnp.sin(twist)
        differ = partner - values
        rot_re = differ[:, 0] * twist_re - differ[:, 1] * twist_im
        rot_im = differ[:, 0] * twist_im + differ[:, 1] * twist_re
        rotated = jnp.stack([rot_re, rot_im], 1)
        values = jnp.where(upper_side == 1, rotated, values + partner)
    residue = reverse_bits(row_place, sections)
    pixel_rows = residue + row_devices * jnp.arange(band_rows, dtype=jnp.int32)
    local_rows = jnp.arange(band_rows, dtype=jnp.int32)
    wrapped_col = pixel_rows[:, None] * local_rows[None, :] % length
    col_angles = wrapped_col.astype(jnp.float32) * (two_pi / length)
    column_table = jnp.stack([jnp.cos(col_angles), -jnp.sin(col_angles)], 1)
    corr = jnp.einsum("tcj,icjw->itw", column_table, values, precision=lax.Precision.HIGHEST)
    corr = corr * (1.0 / (length * tsize_px))
    corr = corr.reshape(mic_count, share_count, band_rows, WCOLS)
    peak_part = jnp.max(corr, axis=1)
    power_part = jnp.sum(corr * corr, axis=1)
    merged = merged_2((peak_part, power_part), "orient", combine_maps)
    return (merged[0][:, None], merged[1][:, None])


def rotation(rows, cols, period):
    angle = np.outer(rows, cols) % period * (two_pi / period)
    return np.cos(angle), np.sin(angle)


def fused_kernel(
    sizes,
    index_ref, spectra_ref, bank_ref,
    enter_hbm, left_hbm, wide_hbm, short_hbm, leave_hbm, column_hbm, twc_hbm, tws_hbm,
    final,
    spec, bank, enter, left, wide, short, leave, column, twc, tws,
    template, own_s, send_s, recv_s, folded, rowpass, tspec, window, prod, p_send, p_all,
    v_all, corr_acc,
    own, sibling, merged,
    spec_sem, load_sem, fold_send, fold_recv, share_send, share_recv, send_sem, recv_sem,
    pair_send, pair_recv, map_send, map_recv, fwd_send, fwd_recv,
):
    bands, share, band, length, tsize = sizes
    half = WCOLS // 2
    hb = band // 2
    full = band + EXTRA
    win = tsize + WCOLS
    hw = win // 2
    me = lax.axis_index("row")
    core = lax.axis_index("orient")
    side = me // 2
    mirror = bands - 1 - me
    level = me + side * (mirror - me)
    peer = me + 1 - 2 * (me % 2)
    starts = [sum(CHUNKS[:k]) for k in range(len(CHUNKS))]
    count = len(CHUNKS)

    def spec_load(mic, k):
        start, n = starts[k], CHUNKS[k]
        row = start + side * (band - 2 * start - n)
        which = (1 - side) if mic == 0 else side
        return pltpu.make_async_copy(
            spectra_ref.at[which, :, pl.ds(pl.multiple_of(row, 16), n), :],
            spec.at[mic, :, pl.ds(start, n), :],
            spec_sem.at[mic, k],
        )

    first_rows = pl.ds(pl.multiple_of(level * band, band), full)
    loads = [
        pltpu.make_async_copy(source, target, load_sem.at[n])
        for n, (source, target) in enumerate(
            [
                (enter_hbm.at[core], enter),
                (bank_ref, bank),
                (left_hbm.at[:, first_rows, :], left),
                (short_hbm, short),
                (wide_hbm, wide),
                (leave_hbm.at[me % 2], leave),
                (column_hbm, column),
                (twc_hbm, twc),
                (tws_hbm, tws),
            ]
        )
    ]
    spec_load(0, 0).start()
    loads[0].start()
    for k in range(1, count):
        spec_load(0, k).start()
    barrier = pltpu.get_barrier_semaphore()
    for k in range(1, bands):
        pl.semaphore_signal(
            barrier, inc=1, device_id={"row": lax.rem(me + k, bands)}, device_id_type=MESH
        )
    pl.semaphore_signal(barrier, inc=1, device_id={"orient": 1 - core}, device_id_type=MESH)

    flip = 1.0 - 2.0 * side.astype(jnp.float32)
    parity = (1 - 2 * core).astype(jnp.bfloat16)

    def chunk_rows(k):
        return pl.ds(starts[k], CHUNKS[k] + (EXTRA if k == count - 1 else 0))

    def fold_copy(k):
        rows = chunk_rows(k)
        return pltpu.make_async_remote_copy(
            src_ref=send_s.at[:, rows, :], dst_ref=recv_s.at[:, rows, :],
            send_sem=fold_send.at[k], recv_sem=fold_recv.at[k],
            device_id={"row": mirror}, device_id_type=MESH,
        )

    def enter_window(mic, target_ref, after):
        carry = jnp.zeros((1, win), jnp.float32)
        for k in range(count):
            start, n = starts[k], CHUNKS[k]
            spec_load(mic, k).wait()
            if mic == 0 and k == 0:
                loads[0].wait()
            low = spec[mic, :, pl.ds(start, n), pl.ds(0, length // 2)]
            high = spec[mic, :, pl.ds(start, n), pl.ds(length // 2, length // 2)]
            mixed = (low + high * parity).reshape(2 * n, length // 2)
            value = jnp.dot(mixed, enter[...], preferred_element_type=jnp.float32)
            real = value[:n, :hw] - value[n:, hw:]
            imag = (value[:n, hw:] + value[n:, :hw]) * flip
            total = jnp.concatenate([real, imag], 1).astype(jnp.bfloat16)
            row_i = lax.broadcasted_iota(jnp.int32, (n, n), 0)
            col_i = lax.broadcasted_iota(jnp.int32, (n, n), 1)
            wanted = row_i + side * ((n - row_i) % n - row_i)
            turn = jnp.where(col_i == wanted, 1.0, 0.0).astype(jnp.bfloat16)
            turned = jnp.dot(turn, total, preferred_element_type=jnp.float32)
            rowid = lax.broadcasted_iota(jnp.int32, (n, win), 0)
            placed = jnp.where(rowid == side - 1, carry, turned).astype(jnp.bfloat16)
            carry = turned[0:1, :]
            for part in range(2):
                target_ref[part, pl.ds(start, n), :] = placed[:, part * hw : (part + 1) * hw]
            if k == count - 1:
                rowid = lax.broadcasted_iota(jnp.int32, (EXTRA, win), 0)
                last = jnp.where(rowid == side - 1, carry, 0.0).astype(jnp.bfloat16)
                for part in range(2):
                    target_ref[part, pl.ds(band, EXTRA), :] = last[:, part * hw : (part + 1) * hw]
            after(k)

    def send_chunk(k):
        if k == 0:
            for later in range(count):
                spec_load(1, later).start()
            pl.semaphore_wait(barrier, bands)
        fold_copy(k).start()
        if k == 0:
            for load in loads[1:]:
                load.start()

    enter_window(0, send_s, send_chunk)
    enter_window(1, own_s, lambda k: None)

    for n in range(1, 4):
        loads[n].wait()
    for o in range(share):
        picture = bank[index_ref[core * share + o]].astype(jnp.float32)
        centred = picture - jnp.mean(picture)
        scale = lax.rsqrt(jnp.mean(centred * centred) + 1e-06)
        template[:, pl.ds(o * tsize, tsize)] = (centred * scale).astype(jnp.bfloat16)
    for part in range(2):
        for o in range(0, share, 2):
            cols = pl.ds(o * tsize, 2 * tsize)
            value = jnp.dot(left[part], template[:, cols], preferred_element_type=jnp.float32)
            rowpass[part, :, cols] = value.astype(jnp.bfloat16)
    for o in range(share):
        cols = pl.ds(o * tsize, tsize)
        for block in range(3):
            step = full // 3
            rows = pl.ds(block * step, step)
            re = jnp.dot(rowpass[0, rows, cols], short[...], preferred_element_type=jnp.float32)
            im = jnp.dot(rowpass[1, rows, cols], short[...], preferred_element_type=jnp.float32)
            tspec[o, rows, pl.ds(0, hw)] = re[:, :hw] + im[:, hw:]
            tspec[o, rows, pl.ds(hw, hw)] = re[:, :hw] - im[:, hw:]
            tspec[o, rows, pl.ds(win, hw)] = im[:, :hw] - re[:, hw:]
            tspec[o, rows, pl.ds(win + hw, hw)] = im[:, :hw] + re[:, hw:]
    for n in range(4, 9):
        loads[n].wait()

    def share_copy(k, source):
        rows = chunk_rows(k)
        return pltpu.make_async_remote_copy(
            src_ref=folded.at[source, :, rows, :], dst_ref=folded.at[source, :, rows, :],
            send_sem=share_send.at[k], recv_sem=share_recv.at[k],
            device_id={"orient": 1 - core}, device_id_type=MESH,
        )

    def part_copy(source, k):
        rows = chunk_rows(k)
        return pltpu.make_async_remote_copy(
            src_ref=p_send.at[:, rows, :], dst_ref=p_all.at[source, :, rows, :],
            send_sem=send_sem.at[k], recv_sem=recv_sem.at[k],
            device_id={"row": peer}, device_id_type=MESH,
        )

    def fold_chunk(k):
        rows = chunk_rows(k)
        fold_copy(k).wait_recv()
        total = own_s[:, rows, :].astype(jnp.float32) + recv_s[:, rows, :].astype(jnp.float32)
        folded[core, :, rows, :] = total.astype(jnp.bfloat16)
        share_copy(k, core).start()

    def product_chunk(k):
        rows = chunk_rows(k)
        n = CHUNKS[k] + (EXTRA if k == count - 1 else 0)
        share_copy(k, 1 - core).wait_recv()
        value = jnp.dot(
            folded[0, :, rows, :].reshape(2 * n, hw), wide[0], preferred_element_type=jnp.float32
        )
        value += jnp.dot(
            folded[1, :, rows, :].reshape(2 * n, hw), wide[1], preferred_element_type=jnp.float32
        )
        re, im = value[:n], value[n:]
        here = pl.ds(0, n)
        window[here, pl.ds(0, hw)] = re[:, :hw] + im[:, hw:]
        window[here, pl.ds(hw, hw)] = re[:, :hw] - im[:, hw:]
        window[here, pl.ds(win, hw)] = im[:, :hw] - re[:, hw:]
        window[here, pl.ds(win + hw, hw)] = im[:, :hw] + re[:, hw:]
        for o in range(share):
            there = pl.ds(o * n, n)
            m_re, m_im = window[here, pl.ds(0, win)], window[here, pl.ds(win, win)]
            t_re, t_im = tspec[o, rows, pl.ds(0, win)], tspec[o, rows, pl.ds(win, win)]
            prod[there, pl.ds(0, win)] = (m_re * t_re + m_im * t_im).astype(jnp.bfloat16)
            prod[there, pl.ds(win, win)] = (m_im * t_re - m_re * t_im).astype(jnp.bfloat16)
        value = jnp.dot(
            prod[pl.ds(0, share * n), :], leave[...], preferred_element_type=jnp.float32
        )
        value = value.astype(jnp.bfloat16)
        for o in range(share):
            p_send[o, rows, :] = value[o * n : (o + 1) * n, WCOLS:]
        part_copy(level, k).start()
        for o in range(share):
            p_all[level, o, rows, :] = value[o * n : (o + 1) * n, :WCOLS]

    factor = 1.0 / (length * tsize * win)

    def column_chunk(k):
        start, n = starts[k], CHUNKS[k]
        rows = pl.ds(start, n)
        part_copy(1 - level, k).wait_recv()
        for o in range(share):
            first = lax.broadcasted_iota(jnp.int32, (n, WCOLS), 1) < half
            b0, b1 = [p_all[b, o, rows, :].astype(jnp.float32) for b in range(2)]
            turned = pltpu.roll(b1, half, 1)
            turned = jnp.where(first, -turned, turned)
            u = [b0 + b1, b0 + turned, b0 - b1, b0 - turned]
            v = [u[0]]
            for rho in range(1, 4):
                span = pl.ds((rho - 1) * WCOLS, WCOLS)
                v.append(u[rho] * twc[rows, span] + pltpu.roll(u[rho], half, 1) * tws[rows, span])
            for pair in range(2):
                even, odd = v[2 * pair], v[2 * pair + 1]
                v_re = jnp.where(first, even, pltpu.roll(odd, half, 1))
                v_im = jnp.where(first, pltpu.roll(even, half, 1), odd)
                span = pl.ds((2 * o + pair) * WCOLS, WCOLS)
                for part, value in enumerate((v_re, v_im)):
                    high = value.astype(jnp.bfloat16)
                    v_all[pl.ds(part * n, n), span] = high
                    v_all[pl.ds((2 + part) * n, n), span] = high
                    v_all[pl.ds((4 + part) * n, n), span] = (
                        value - high.astype(jnp.float32)
                    ).astype(jnp.bfloat16)
        table = column[:, pl.ds(6 * start, 6 * n)]
        corr = jnp.dot(table, v_all[pl.ds(0, 6 * n), :], preferred_element_type=jnp.float32)
        if k == 0:
            corr_acc[...] = corr
        else:
            corr_acc[...] += corr

    for k in range(count):
        fold_chunk(k)
        if k > 0:
            column_chunk(k - 1)
        product_chunk(k)
    column_chunk(count - 1)

    edge = []
    for o in range(share):
        e0, e1 = [p_all[b, o, pl.ds(band, EXTRA), :].astype(jnp.float32) for b in range(2)]
        first = lax.broadcasted_iota(jnp.int32, (EXTRA, WCOLS), 1) < half
        swapped_0, swapped_1 = pltpu.roll(e0, half, 1), pltpu.roll(e1, half, 1)
        edge.append(
            [
                jnp.where(first, e0 + e1, -e0 - swapped_1)[0:1, :],
                jnp.where(first, e1 - e0, e0 - swapped_1)[0:1, :],
            ]
        )

    first = lax.broadcasted_iota(jnp.int32, (band, WCOLS), 1) < half
    for pair in range(2):
        hi = po = None
        for o in range(share):
            corr = (corr_acc[:, pl.ds((2 * o + pair) * WCOLS, WCOLS)] + edge[o][pair]) * factor
            hi = corr if o == 0 else jnp.maximum(hi, corr)
            po = corr * corr if o == 0 else po + corr * corr
        own[pair] = jnp.where(first, hi, pltpu.roll(po, half, 1))
        own[pair + 2] = jnp.where(first, pltpu.roll(hi, half, 1), po)

    mine = pl.ds(pl.multiple_of(core * hb, hb), hb)
    theirs = pl.ds(pl.multiple_of((1 - core) * hb, hb), hb)

    def swap(k):
        q = lax.rem(me + k, bands)
        return pltpu.make_async_remote_copy(
            src_ref=own.at[q, theirs, :], dst_ref=sibling.at[q],
            send_sem=pair_send.at[k], recv_sem=pair_recv.at[k],
            device_id={"orient": 1 - core}, device_id_type=MESH,
        )

    for k in (2, 1, 3, 0):
        swap(k).start()
    first = lax.broadcasted_iota(jnp.int32, (hb, WCOLS), 1) < half

    def map_copy(k, source):
        dest = lax.rem(me + k, bands)
        return pltpu.make_async_remote_copy(
            src_ref=merged.at[dest], dst_ref=final.at[source, mine, :],
            send_sem=map_send.at[k], recv_sem=map_recv.at[source],
            device_id={"row": dest}, device_id_type=MESH,
        )

    def forward(source, rows):
        return pltpu.make_async_remote_copy(
            src_ref=final.at[source, rows, :], dst_ref=final.at[source, rows, :],
            send_sem=fwd_send.at[source], recv_sem=fwd_recv.at[source],
            device_id={"orient": 1 - core}, device_id_type=MESH,
        )

    for k in (2, 1, 3, 0):
        swap(k).wait_recv()
        q = lax.rem(me + k, bands)
        one, two = own[q, mine, :], sibling[q]
        total = jnp.where(first, jnp.maximum(one, two), one + two).astype(final.dtype)
        if k == 0:
            final[me, mine, :] = total
        else:
            merged[q] = total
            map_copy(k, me).start()
    forward(me, mine).start()
    for k in (1, 3, 2):
        source = lax.rem(me + k, bands)
        map_copy(k, source).wait_recv()
        forward(source, mine).start()
    for source in range(4):
        forward(source, theirs).wait_recv()
    for source in range(4):
        forward(source, mine).wait_send()
    for k in range(1, bands):
        map_copy(k, me).wait_send()
    for k in range(bands):
        swap(k).wait_send()
    for k in range(count):
        fold_copy(k).wait_send()
        share_copy(k, core).wait_send()
        part_copy(level, k).wait_send()


def assemble_kernel(maps, peak_ref, power_ref):
    half = WCOLS // 2
    first = lax.broadcasted_iota(jnp.int32, maps.shape[1:], 1) < half
    a, b = maps[0].astype(jnp.float32), maps[1].astype(jnp.float32)
    peak_ref[0, 0] = jnp.where(first, a, pltpu.roll(b, half, 1))
    power_ref[0, 0] = jnp.where(first, pltpu.roll(a, half, 1), b)


def shards_fused(spectra, bank, orient_index):
    band = spectra.shape[2]
    length = spectra.shape[3]
    tsize = bank.shape[1]
    bands = lax.axis_size("row")
    share = orient_index.shape[0] // lax.axis_size("orient")
    half = WCOLS // 2
    win = tsize + WCOLS
    hw = win // 2
    count = len(CHUNKS)
    full = band + EXTRA
    bf, f32 = jnp.bfloat16, jnp.float32

    def low(table):
        return np.ascontiguousarray(table).astype(np.float32).astype(bf)

    def blocks(re, im):
        return np.concatenate([np.concatenate([re, im], 1), np.concatenate([-im, re], 1)], 0)

    kx = np.arange(length // 2)
    place = np.arange(hw)
    enter = np.stack([np.concatenate(rotation(kx, 2 * place + c, length), 1) for c in range(2)])
    ky = np.arange(2 * band + EXTRA)
    cos_y, sin_y = rotation(ky, np.arange(tsize), length)
    left = np.stack([cos_y, -sin_y])
    freq = np.arange(hw) + 0.5
    wide = np.stack([np.concatenate(rotation(2 * place + c, freq, win), 1) for c in range(2)])
    short = np.concatenate(rotation(np.arange(tsize), freq, win), 1)
    both = np.concatenate([freq, -freq])
    leave = []
    for xh in range(2):
        tiles = []
        for h in (xh, 1 - xh):
            tiles.append(blocks(*rotation(both, h * half + np.arange(half), win)))
        leave.append(np.concatenate(tiles, 1))
    leave = np.stack(leave)
    column = []
    for k, n in enumerate(CHUNKS):
        col_j = sum(CHUNKS[:k]) + np.arange(n)
        cos_c, sin_c = rotation(np.arange(band), col_j, band)
        exact = np.concatenate([cos_c, -sin_c], 1).astype(np.float32)
        high = low(exact).astype(np.float32)
        column += [high, exact - high, high]
    column = np.concatenate(column, 1)
    rho = np.repeat(np.arange(1, 4), WCOLS)
    twc, tws = rotation(np.arange(band), rho, length)
    tws = np.where(np.arange(3 * WCOLS) % WCOLS < half, -tws, tws)
    tables = [
        low(enter), low(left), low(wide), low(short), low(leave), low(column),
        twc.astype(np.float32), tws.astype(np.float32),
    ]
    vmem = pl.BlockSpec(memory_space=pltpu.VMEM)
    hbm = pl.BlockSpec(memory_space=pl.ANY)
    dma = pltpu.SemaphoreType.DMA
    maps = pl.pallas_call(
        functools.partial(fused_kernel, (bands, share, band, length, tsize)),
        out_shape=jax.ShapeDtypeStruct((4, band, WCOLS), MAPS),
        in_specs=[pl.BlockSpec(memory_space=pltpu.SMEM)] + [hbm] * (2 + len(tables)),
        out_specs=vmem,
        scratch_shapes=[
            pltpu.VMEM(spectra.shape, bf),
            pltpu.VMEM(bank.shape, bf),
            pltpu.VMEM((length // 2, win), bf),
            pltpu.VMEM((2, full, tsize), bf),
            pltpu.VMEM((2, hw, win), bf),
            pltpu.VMEM((tsize, win), bf),
            pltpu.VMEM((2 * win, 2 * WCOLS), bf),
            pltpu.VMEM((band, 6 * band), bf),
            pltpu.VMEM((band, 3 * WCOLS), f32),
            pltpu.VMEM((band, 3 * WCOLS), f32),
            pltpu.VMEM((tsize, share * tsize), bf),
            pltpu.VMEM((2, full, hw), bf),
            pltpu.VMEM((2, full, hw), bf),
            pltpu.VMEM((2, full, hw), bf),
            pltpu.VMEM((2, 2, full, hw), bf),
            pltpu.VMEM((2, full, share * tsize), bf),
            pltpu.VMEM((share, full, 2 * win), f32),
            pltpu.VMEM((max(CHUNKS) + EXTRA, 2 * win), f32),
            pltpu.VMEM((share * (max(CHUNKS) + EXTRA), 2 * win), bf),
            pltpu.VMEM((share, full, WCOLS), bf),
            pltpu.VMEM((2, share, full, WCOLS), bf),
            pltpu.VMEM((6 * max(CHUNKS), 2 * share * WCOLS), bf),
            pltpu.VMEM((band, 2 * share * WCOLS), f32),
            pltpu.VMEM((4, band, WCOLS), f32),
            pltpu.VMEM((4, band // 2, WCOLS), f32),
            pltpu.VMEM((4, band // 2, WCOLS), MAPS),
            dma((2, count)),
            dma((9,)),
            dma((count,)),
            dma((count,)),
            dma((count,)),
            dma((count,)),
            dma((count,)),
            dma((count,)),
            dma((bands,)),
            dma((bands,)),
            dma((bands,)),
            dma((bands,)),
            dma((bands,)),
            dma((bands,)),
        ],
        compiler_params=pltpu.CompilerParams(
            collective_id=0, has_side_effects=True, vmem_limit_bytes=58 << 20
        ),
    )(orient_index, spectra, bank, *tables)
    out = jax.ShapeDtypeStruct((2, 1, band, WCOLS), f32)
    one_mic = pl.BlockSpec((1, 1, band, WCOLS), lambda m: (m, 0, 0, 0))
    return pl.pallas_call(
        assemble_kernel,
        grid=(2,),
        out_shape=(out, out),
        in_specs=[pl.BlockSpec((2, band, WCOLS), lambda m: (m, 0, 0))],
        out_specs=(one_mic, one_mic),
    )(maps)


def shards(spectra, bank, orient_index):
    fits = (
        lax.axis_size("row") == 4
        and lax.axis_size("orient") == 2
        and spectra.shape[0] == 2
        and spectra.shape[2] == 4 * WCOLS
        and bank.shape[1] == 3 * WCOLS
        and spectra.shape[3] == 4 * spectra.shape[2]
    )
    body = shards_fused if fits else shards_general
    return body(spectra, bank, orient_index)


def solution(mesh):
    return jax.shard_map(
        shards,
        mesh=mesh,
        in_specs=(P(("grp", "mic"), None, "row", None), P(), P("grp")),
        out_specs=(P(("grp", "mic"), "row", None, None), P(("grp", "mic"), "row", None, None)),
        check_vma=False,
    )
```

```python
import functools
import math

import jax
import jax.numpy as jnp
import numpy as np
from jax import lax
from jax.experimental import pallas as pl
from jax.experimental.pallas import tpu as pltpu
from jax.sharding import PartitionSpec as P

WCOLS = 128
MESH = pl.DeviceIdType.MESH
EXTRA = 16
MAPS = jnp.bfloat16
CHUNKS = (64, 128, 128, 128, 64)
ORDER = (2, 3, 1, 0)


two_pi = 2.0 * math.pi


def swapped(shard, axis, apart):
    return lax.ppermute(shard, axis, [(i, i ^ 1 << apart) for i in range(lax.axis_size(axis))])


def merged_2(part, axis, combine):
    gathered = jax.tree.map(lambda a: lax.all_gather(a, axis), part)

    def take(source):
        return jax.tree.map(lambda a: lax.dynamic_index_in_dim(a, source, 0, False), gathered)

    return lax.fori_loop(
        1, lax.axis_size(axis), lambda source, state: combine(state, take(source)), take(0)
    )


def phase_table(row_start, row_count, col_start, col_count, period):
    row_ids = row_start + jnp.arange(row_count, dtype=jnp.int32)
    col_ids = col_start + jnp.arange(col_count, dtype=jnp.int32)
    wrapped = row_ids[:, None] * col_ids[None, :] % period
    angles = wrapped.astype(jnp.float32) * (two_pi / period)
    return (jnp.cos(angles), jnp.sin(angles))


def normalize(picture):
    values = picture.astype(jnp.float32)
    centred = values - jnp.mean(values)
    factor = lax.rsqrt(jnp.mean(centred * centred) + 1e-06)
    return (centred * factor).astype(jnp.bfloat16)


def reverse_bits(number, digits):
    result = number * 0
    for digit in range(digits):
        result = result + number // (1 << digit) % 2 * (1 << digits - 1 - digit)
    return result


def combine_maps(first_pair, second_pair):
    return (jnp.maximum(first_pair[0], second_pair[0]), first_pair[1] + second_pair[1])


def shards_general(spectra, bank, orient_index):
    mic_count = spectra.shape[0]
    band_rows = spectra.shape[2]
    length = spectra.shape[3]
    tsize_px = bank.shape[1]
    row_devices = lax.axis_size("row")
    row_place = lax.axis_index("row")
    share_count = orient_index.shape[0] // lax.axis_size("orient")
    chosen = lax.dynamic_slice_in_dim(
        orient_index, lax.axis_index("orient") * share_count, share_count
    )
    templates = jnp.stack(
        [
            normalize(lax.dynamic_index_in_dim(bank, chosen[place], 0, False))
            for place in range(share_count)
        ]
    )
    cos_y, sin_y = phase_table(row_place * band_rows, band_rows, 0, tsize_px, length)
    left_table = jnp.concatenate([cos_y.astype(jnp.bfloat16), -sin_y.astype(jnp.bfloat16)], 0)
    rowpass = jnp.einsum(
        "ay,oyx->oax", left_table, templates, preferred_element_type=jnp.float32
    ).astype(jnp.bfloat16)
    cos_x, sin_x = phase_table(0, tsize_px, 0, length, length)
    right_table = jnp.concatenate([cos_x.astype(jnp.bfloat16), sin_x.astype(jnp.bfloat16)], 1)
    mixed = jnp.einsum("oax,xk->oak", rowpass, right_table, preferred_element_type=jnp.float32)
    upper_rows = mixed[:, :band_rows]
    lower_rows = mixed[:, band_rows:]
    spec_re = upper_rows[:, :, :length] + lower_rows[:, :, length:]
    spec_im = lower_rows[:, :, :length] - upper_rows[:, :, length:]
    piece = jnp.stack([spec_re, spec_im], 1).astype(jnp.bfloat16)
    cos_e, sin_e = phase_table(0, length, 0, WCOLS, length)
    row_table = jnp.concatenate([cos_e.astype(jnp.bfloat16), sin_e.astype(jnp.bfloat16)], 1)
    updates = []
    for orient_pos in range(share_count):
        tmpl_re = piece[orient_pos, 0].astype(jnp.float32)
        tmpl_im = piece[orient_pos, 1].astype(jnp.float32)
        mic_re = spectra[:, 0].astype(jnp.float32)
        mic_im = spectra[:, 1].astype(jnp.float32)
        prod_re = mic_re * tmpl_re + mic_im * tmpl_im
        prod_im = mic_im * tmpl_re - mic_re * tmpl_im
        product = jnp.stack([prod_re, prod_im], 1).astype(jnp.bfloat16)
        summed = jnp.einsum("mcbk,kw->mcbw", product, row_table, preferred_element_type=jnp.float32)
        part_re = summed[:, 0, :, :WCOLS] - summed[:, 1, :, WCOLS:]
        part_im = summed[:, 0, :, WCOLS:] + summed[:, 1, :, :WCOLS]
        updates.append(jnp.stack([part_re, part_im], 1))
    partial_value = jnp.stack(updates, 1)
    item_total = mic_count * share_count
    values = partial_value.reshape(item_total, 2, band_rows, WCOLS)
    sections = row_devices.bit_length() - 1
    for bit in reversed(range(sections)):
        half_span = 1 << bit
        partner = swapped(values, "row", bit)
        upper_side = row_place // half_span % 2
        offset = row_place % half_span
        twist = offset.astype(jnp.float32) * (math.pi / half_span)
        twist_re = jnp.cos(twist)
        twist_im = jnp.sin(twist)
        differ = partner - values
        rot_re = differ[:, 0] * twist_re - differ[:, 1] * twist_im
        rot_im = differ[:, 0] * twist_im + differ[:, 1] * twist_re
        rotated = jnp.stack([rot_re, rot_im], 1)
        values = jnp.where(upper_side == 1, rotated, values + partner)
    residue = reverse_bits(row_place, sections)
    pixel_rows = residue + row_devices * jnp.arange(band_rows, dtype=jnp.int32)
    local_rows = jnp.arange(band_rows, dtype=jnp.int32)
    wrapped_col = pixel_rows[:, None] * local_rows[None, :] % length
    col_angles = wrapped_col.astype(jnp.float32) * (two_pi / length)
    column_table = jnp.stack([jnp.cos(col_angles), -jnp.sin(col_angles)], 1)
    corr = jnp.einsum("tcj,icjw->itw", column_table, values, precision=lax.Precision.HIGHEST)
    corr = corr * (1.0 / (length * tsize_px))
    corr = corr.reshape(mic_count, share_count, band_rows, WCOLS)
    peak_part = jnp.max(corr, axis=1)
    power_part = jnp.sum(corr * corr, axis=1)
    merged = merged_2((peak_part, power_part), "orient", combine_maps)
    return (merged[0][:, None], merged[1][:, None])


def rotation(rows, cols, period):
    angle = np.outer(rows, cols) % period * (two_pi / period)
    return np.cos(angle), np.sin(angle)


def fused_kernel(
    sizes,
    index_hbm, spectra_ref, bank_ref,
    enter_hbm, left_hbm, wide_hbm, short_hbm, leave_hbm, column_hbm, twc_hbm, tws_hbm,
    final,
    index, spec, bank, enter, left, wide, short, leave, column, twc, tws,
    template, own_s, send_s, recv_s, folded, rowpass, tspec, window, prod, p_send, p_all,
    v_all, corr_acc,
    own, sibling, merged,
    spec_sem, load_sem, fold_send, fold_recv, share_send, share_recv, send_sem, recv_sem,
    pair_send, pair_recv, map_send, map_recv, fwd_send, fwd_recv,
):
    bands, share, band, length, tsize = sizes
    half = WCOLS // 2
    hb = band // 2
    full = band + EXTRA
    win = tsize + WCOLS
    hw = win // 2
    me = lax.axis_index("row")
    core = lax.axis_index("orient")
    side = me // 2
    mirror = bands - 1 - me
    level = me + side * (mirror - me)
    peer = me + 1 - 2 * (me % 2)
    starts = [sum(CHUNKS[:k]) for k in range(len(CHUNKS))]
    count = len(CHUNKS)

    def spec_load(mic, k):
        start, n = starts[k], CHUNKS[k]
        row = start + side * (band - 2 * start - n)
        which = (1 - side) if mic == 0 else side
        return pltpu.make_async_copy(
            spectra_ref.at[which, :, pl.ds(pl.multiple_of(row, 16), n), :],
            spec.at[mic, :, pl.ds(start, n), :],
            spec_sem.at[mic, k],
        )

    first_rows = pl.ds(pl.multiple_of(level * band, band), full)
    loads = [
        pltpu.make_async_copy(source, target, load_sem.at[n])
        for n, (source, target) in enumerate(
            [
                (enter_hbm.at[core], enter),
                (bank_ref, bank),
                (left_hbm.at[:, first_rows, :], left),
                (short_hbm, short),
                (wide_hbm, wide),
                (leave_hbm.at[me % 2], leave),
                (column_hbm, column),
                (twc_hbm, twc),
                (tws_hbm, tws),
                (index_hbm, index),
            ]
        )
    ]
    spec_load(0, 0).start()
    loads[0].start()
    for k in range(1, count):
        spec_load(0, k).start()
    for k in range(count):
        spec_load(1, k).start()
    for load in loads[1:]:
        load.start()
    barrier = pltpu.get_barrier_semaphore()
    for k in range(1, bands):
        pl.semaphore_signal(
            barrier, inc=1, device_id={"row": lax.rem(me + k, bands)}, device_id_type=MESH
        )
    pl.semaphore_signal(barrier, inc=1, device_id={"orient": 1 - core}, device_id_type=MESH)

    flip = 1.0 - 2.0 * side.astype(jnp.float32)
    parity = (1 - 2 * core).astype(jnp.bfloat16)

    def chunk_rows(k):
        return pl.ds(starts[k], CHUNKS[k] + (EXTRA if k == count - 1 else 0))

    def fold_copy(k):
        rows = chunk_rows(k)
        return pltpu.make_async_remote_copy(
            src_ref=send_s.at[:, rows, :], dst_ref=recv_s.at[:, rows, :],
            send_sem=fold_send.at[k], recv_sem=fold_recv.at[k],
            device_id={"row": mirror}, device_id_type=MESH,
        )

    def enter_window(mic, target_ref, ks, carry):
        for k in ks:
            start, n = starts[k], CHUNKS[k]
            spec_load(mic, k).wait()
            if mic == 0 and k == 0:
                loads[0].wait()
            low = spec[mic, :, pl.ds(start, n), pl.ds(0, length // 2)]
            high = spec[mic, :, pl.ds(start, n), pl.ds(length // 2, length // 2)]
            mixed = (low + high * parity).reshape(2 * n, length // 2)
            value = jnp.dot(mixed, enter[...], preferred_element_type=jnp.float32)
            real = value[:n, :hw] - value[n:, hw:]
            imag = (value[:n, hw:] + value[n:, :hw]) * flip
            total = jnp.concatenate([real, imag], 1).astype(jnp.bfloat16)
            row_i = lax.broadcasted_iota(jnp.int32, (n, n), 0)
            col_i = lax.broadcasted_iota(jnp.int32, (n, n), 1)
            wanted = row_i + side * ((n - row_i) % n - row_i)
            turn = jnp.where(col_i == wanted, 1.0, 0.0).astype(jnp.bfloat16)
            turned = jnp.dot(turn, total, preferred_element_type=jnp.float32)
            rowid = lax.broadcasted_iota(jnp.int32, (n, win), 0)
            placed = jnp.where(rowid == side - 1, carry, turned).astype(jnp.bfloat16)
            carry = turned[0:1, :]
            for part in range(2):
                target_ref[part, pl.ds(start, n), :] = placed[:, part * hw : (part + 1) * hw]
            if k == count - 1:
                rowid = lax.broadcasted_iota(jnp.int32, (EXTRA, win), 0)
                last = jnp.where(rowid == side - 1, carry, 0.0).astype(jnp.bfloat16)
                for part in range(2):
                    target_ref[part, pl.ds(band, EXTRA), :] = last[:, part * hw : (part + 1) * hw]
            if mic == 0:
                send_chunk(k)
        return carry

    def send_chunk(k):
        if k == 0:
            pl.semaphore_wait(barrier, bands)
        fold_copy(k).start()

    blank = jnp.zeros((1, win), jnp.float32)
    enter_window(0, send_s, range(count), blank)

    for n in (1, 2, 3, 9):
        loads[n].wait()
    for o in range(share):
        picture = bank[index[core * share + o]].astype(jnp.float32)
        centred = picture - jnp.mean(picture)
        scale = lax.rsqrt(jnp.mean(centred * centred) + 1e-06)
        template[:, pl.ds(o * tsize, tsize)] = (centred * scale).astype(jnp.bfloat16)
    for part in range(2):
        for o in range(0, share, 2):
            cols = pl.ds(o * tsize, 2 * tsize)
            value = jnp.dot(left[part], template[:, cols], preferred_element_type=jnp.float32)
            rowpass[part, :, cols] = value.astype(jnp.bfloat16)
    for o in range(share):
        cols = pl.ds(o * tsize, tsize)
        for block in range(3):
            step = full // 3
            rows = pl.ds(block * step, step)
            re = jnp.dot(rowpass[0, rows, cols], short[...], preferred_element_type=jnp.float32)
            im = jnp.dot(rowpass[1, rows, cols], short[...], preferred_element_type=jnp.float32)
            tspec[o, rows, pl.ds(0, hw)] = re[:, :hw] + im[:, hw:]
            tspec[o, rows, pl.ds(hw, hw)] = re[:, :hw] - im[:, hw:]
            tspec[o, rows, pl.ds(win, hw)] = im[:, :hw] - re[:, hw:]
            tspec[o, rows, pl.ds(win + hw, hw)] = im[:, :hw] + re[:, hw:]
    for n in range(4, 9):
        loads[n].wait()

    def share_copy(k, source):
        rows = chunk_rows(k)
        return pltpu.make_async_remote_copy(
            src_ref=folded.at[source, :, rows, :], dst_ref=folded.at[source, :, rows, :],
            send_sem=share_send.at[k], recv_sem=share_recv.at[k],
            device_id={"orient": 1 - core}, device_id_type=MESH,
        )

    def part_copy(source, k):
        rows = chunk_rows(k)
        return pltpu.make_async_remote_copy(
            src_ref=p_send.at[:, rows, :], dst_ref=p_all.at[source, :, rows, :],
            send_sem=send_sem.at[k], recv_sem=recv_sem.at[k],
            device_id={"row": peer}, device_id_type=MESH,
        )

    def fold_chunk(k):
        rows = chunk_rows(k)
        fold_copy(k).wait_recv()
        total = own_s[:, rows, :].astype(jnp.float32) + recv_s[:, rows, :].astype(jnp.float32)
        folded[core, :, rows, :] = total.astype(jnp.bfloat16)
        share_copy(k, core).start()

    def product_chunk(k):
        rows = chunk_rows(k)
        n = CHUNKS[k] + (EXTRA if k == count - 1 else 0)
        share_copy(k, 1 - core).wait_recv()
        value = jnp.dot(
            folded[0, :, rows, :].reshape(2 * n, hw), wide[0], preferred_element_type=jnp.float32
        )
        value += jnp.dot(
            folded[1, :, rows, :].reshape(2 * n, hw), wide[1], preferred_element_type=jnp.float32
        )
        re, im = value[:n], value[n:]
        here = pl.ds(0, n)
        window[here, pl.ds(0, hw)] = re[:, :hw] + im[:, hw:]
        window[here, pl.ds(hw, hw)] = re[:, :hw] - im[:, hw:]
        window[here, pl.ds(win, hw)] = im[:, :hw] - re[:, hw:]
        window[here, pl.ds(win + hw, hw)] = im[:, :hw] + re[:, hw:]
        for o in range(share):
            there = pl.ds(o * n, n)
            m_re, m_im = window[here, pl.ds(0, win)], window[here, pl.ds(win, win)]
            t_re, t_im = tspec[o, rows, pl.ds(0, win)], tspec[o, rows, pl.ds(win, win)]
            prod[there, pl.ds(0, win)] = (m_re * t_re + m_im * t_im).astype(jnp.bfloat16)
            prod[there, pl.ds(win, win)] = (m_im * t_re - m_re * t_im).astype(jnp.bfloat16)
        value = jnp.dot(
            prod[pl.ds(0, share * n), :], leave[...], preferred_element_type=jnp.float32
        )
        value = value.astype(jnp.bfloat16)
        for o in range(share):
            p_send[o, rows, :] = value[o * n : (o + 1) * n, WCOLS:]
        part_copy(level, k).start()
        for o in range(share):
            p_all[level, o, rows, :] = value[o * n : (o + 1) * n, :WCOLS]

    factor = 1.0 / (length * tsize * win)

    def column_chunk(k):
        start, n = starts[k], CHUNKS[k]
        rows = pl.ds(start, n)
        part_copy(1 - level, k).wait_recv()
        for o in range(share):
            first = lax.broadcasted_iota(jnp.int32, (n, WCOLS), 1) < half
            b0, b1 = [p_all[b, o, rows, :].astype(jnp.float32) for b in range(2)]
            turned = pltpu.roll(b1, half, 1)
            turned = jnp.where(first, -turned, turned)
            u = [b0 + b1, b0 + turned, b0 - b1, b0 - turned]
            v = [u[0]]
            for rho in range(1, 4):
                span = pl.ds((rho - 1) * WCOLS, WCOLS)
                v.append(u[rho] * twc[rows, span] + pltpu.roll(u[rho], half, 1) * tws[rows, span])
            for pair in range(2):
                even, odd = v[2 * pair], v[2 * pair + 1]
                v_re = jnp.where(first, even, pltpu.roll(odd, half, 1))
                v_im = jnp.where(first, pltpu.roll(even, half, 1), odd)
                span = pl.ds((2 * o + pair) * WCOLS, WCOLS)
                for part, value in enumerate((v_re, v_im)):
                    v_all[pl.ds(part * n, n), span] = value.astype(jnp.bfloat16)
        table = column[:, pl.ds(2 * start, 2 * n)]
        corr = jnp.dot(table, v_all[pl.ds(0, 2 * n), :], preferred_element_type=jnp.float32)
        if k == 0:
            corr_acc[...] = corr
        else:
            corr_acc[...] += corr

    carried = blank
    for k in range(count):
        carried = enter_window(1, own_s, (k,), carried)
        fold_chunk(k)
        if k > 1:
            column_chunk(k - 2)
        product_chunk(k)
    column_chunk(count - 2)
    column_chunk(count - 1)

    edge = []
    for o in range(share):
        e0, e1 = [p_all[b, o, pl.ds(band, EXTRA), :].astype(jnp.float32) for b in range(2)]
        first = lax.broadcasted_iota(jnp.int32, (EXTRA, WCOLS), 1) < half
        swapped_0, swapped_1 = pltpu.roll(e0, half, 1), pltpu.roll(e1, half, 1)
        edge.append(
            [
                jnp.where(first, e0 + e1, -e0 - swapped_1)[0:1, :],
                jnp.where(first, e1 - e0, e0 - swapped_1)[0:1, :],
            ]
        )

    first = lax.broadcasted_iota(jnp.int32, (band, WCOLS), 1) < half
    for pair in range(2):
        hi = po = None
        for o in range(share):
            corr = (corr_acc[:, pl.ds((2 * o + pair) * WCOLS, WCOLS)] + edge[o][pair]) * factor
            hi = corr if o == 0 else jnp.maximum(hi, corr)
            po = corr * corr if o == 0 else po + corr * corr
        own[pair] = jnp.where(first, hi, pltpu.roll(po, half, 1))
        own[pair + 2] = jnp.where(first, pltpu.roll(hi, half, 1), po)

    mine = pl.ds(pl.multiple_of(core * hb, hb), hb)
    theirs = pl.ds(pl.multiple_of((1 - core) * hb, hb), hb)

    def target_of(k):
        if k == 0:
            return me
        return peer if k == 1 else (1 - side) * 2 + (k - 2 + me) % 2

    def swap(k):
        q = target_of(k)
        return pltpu.make_async_remote_copy(
            src_ref=own.at[q, theirs, :], dst_ref=sibling.at[q],
            send_sem=pair_send.at[k], recv_sem=pair_recv.at[k],
            device_id={"orient": 1 - core}, device_id_type=MESH,
        )

    for k in ORDER:
        swap(k).start()
    first = lax.broadcasted_iota(jnp.int32, (hb, WCOLS), 1) < half

    def map_copy(k, source):
        dest = target_of(k)
        return pltpu.make_async_remote_copy(
            src_ref=merged.at[dest], dst_ref=final.at[source, mine, :],
            send_sem=map_send.at[k], recv_sem=map_recv.at[source],
            device_id={"row": dest}, device_id_type=MESH,
        )

    def forward(source, rows):
        return pltpu.make_async_remote_copy(
            src_ref=final.at[source, rows, :], dst_ref=final.at[source, rows, :],
            send_sem=fwd_send.at[source], recv_sem=fwd_recv.at[source],
            device_id={"orient": 1 - core}, device_id_type=MESH,
        )

    for k in ORDER:
        swap(k).wait_recv()
        q = target_of(k)
        one, two = own[q, mine, :], sibling[q]
        total = jnp.where(first, jnp.maximum(one, two), one + two).astype(final.dtype)
        if k == 0:
            final[me, mine, :] = total
        else:
            merged[q] = total
            map_copy(k, me).start()
    forward(me, mine).start()
    for k in (1, 2, 3):
        source = target_of(k)
        map_copy(k, source).wait_recv()
        forward(source, mine).start()
    for source in range(4):
        forward(source, theirs).wait_recv()
    for source in range(4):
        forward(source, mine).wait_send()
    for k in range(1, bands):
        map_copy(k, me).wait_send()
    for k in range(bands):
        swap(k).wait_send()
    for k in range(count):
        fold_copy(k).wait_send()
        share_copy(k, core).wait_send()
        part_copy(level, k).wait_send()


def assemble_kernel(maps, peak_ref, power_ref):
    half = WCOLS // 2
    first = lax.broadcasted_iota(jnp.int32, maps.shape[1:], 1) < half
    a, b = maps[0].astype(jnp.float32), maps[1].astype(jnp.float32)
    peak_ref[0, 0] = jnp.where(first, a, pltpu.roll(b, half, 1))
    power_ref[0, 0] = jnp.where(first, pltpu.roll(a, half, 1), b)


def shards_fused(spectra, bank, orient_index):
    band = spectra.shape[2]
    length = spectra.shape[3]
    tsize = bank.shape[1]
    bands = lax.axis_size("row")
    share = orient_index.shape[0] // lax.axis_size("orient")
    half = WCOLS // 2
    win = tsize + WCOLS
    hw = win // 2
    count = len(CHUNKS)
    full = band + EXTRA
    bf, f32 = jnp.bfloat16, jnp.float32

    def low(table):
        return np.ascontiguousarray(table).astype(np.float32).astype(bf)

    def blocks(re, im):
        return np.concatenate([np.concatenate([re, im], 1), np.concatenate([-im, re], 1)], 0)

    kx = np.arange(length // 2)
    place = np.arange(hw)
    enter = np.stack([np.concatenate(rotation(kx, 2 * place + c, length), 1) for c in range(2)])
    ky = np.arange(2 * band + EXTRA)
    cos_y, sin_y = rotation(ky, np.arange(tsize), length)
    left = np.stack([cos_y, -sin_y])
    freq = np.arange(hw) + 0.5
    wide = np.stack([np.concatenate(rotation(2 * place + c, freq, win), 1) for c in range(2)])
    short = np.concatenate(rotation(np.arange(tsize), freq, win), 1)
    both = np.concatenate([freq, -freq])
    leave = []
    for xh in range(2):
        tiles = []
        for h in (xh, 1 - xh):
            tiles.append(blocks(*rotation(both, h * half + np.arange(half), win)))
        leave.append(np.concatenate(tiles, 1))
    leave = np.stack(leave)
    column = []
    for k, n in enumerate(CHUNKS):
        col_j = sum(CHUNKS[:k]) + np.arange(n)
        cos_c, sin_c = rotation(np.arange(band), col_j, band)
        column += [cos_c, -sin_c]
    column = np.concatenate(column, 1)
    rho = np.repeat(np.arange(1, 4), WCOLS)
    twc, tws = rotation(np.arange(band), rho, length)
    tws = np.where(np.arange(3 * WCOLS) % WCOLS < half, -tws, tws)
    tables = [
        low(enter), low(left), low(wide), low(short), low(leave), low(column),
        twc.astype(np.float32), tws.astype(np.float32),
    ]
    vmem = pl.BlockSpec(memory_space=pltpu.VMEM)
    hbm = pl.BlockSpec(memory_space=pl.ANY)
    dma = pltpu.SemaphoreType.DMA
    maps = pl.pallas_call(
        functools.partial(fused_kernel, (bands, share, band, length, tsize)),
        out_shape=jax.ShapeDtypeStruct((4, band, WCOLS), MAPS),
        in_specs=[hbm] * (3 + len(tables)),
        out_specs=vmem,
        scratch_shapes=[
            pltpu.SMEM(orient_index.shape, jnp.int32),
            pltpu.VMEM(spectra.shape, bf),
            pltpu.VMEM(bank.shape, bf),
            pltpu.VMEM((length // 2, win), bf),
            pltpu.VMEM((2, full, tsize), bf),
            pltpu.VMEM((2, hw, win), bf),
            pltpu.VMEM((tsize, win), bf),
            pltpu.VMEM((2 * win, 2 * WCOLS), bf),
            pltpu.VMEM((band, 2 * band), bf),
            pltpu.VMEM((band, 3 * WCOLS), f32),
            pltpu.VMEM((band, 3 * WCOLS), f32),
            pltpu.VMEM((tsize, share * tsize), bf),
            pltpu.VMEM((2, full, hw), bf),
            pltpu.VMEM((2, full, hw), bf),
            pltpu.VMEM((2, full, hw), bf),
            pltpu.VMEM((2, 2, full, hw), bf),
            pltpu.VMEM((2, full, share * tsize), bf),
            pltpu.VMEM((share, full, 2 * win), f32),
            pltpu.VMEM((max(CHUNKS) + EXTRA, 2 * win), f32),
            pltpu.VMEM((share * (max(CHUNKS) + EXTRA), 2 * win), bf),
            pltpu.VMEM((share, full, WCOLS), bf),
            pltpu.VMEM((2, share, full, WCOLS), bf),
            pltpu.VMEM((2 * max(CHUNKS), 2 * share * WCOLS), bf),
            pltpu.VMEM((band, 2 * share * WCOLS), f32),
            pltpu.VMEM((4, band, WCOLS), f32),
            pltpu.VMEM((4, band // 2, WCOLS), f32),
            pltpu.VMEM((4, band // 2, WCOLS), MAPS),
            dma((2, count)),
            dma((10,)),
            dma((count,)),
            dma((count,)),
            dma((count,)),
            dma((count,)),
            dma((count,)),
            dma((count,)),
            dma((bands,)),
            dma((bands,)),
            dma((bands,)),
            dma((bands,)),
            dma((bands,)),
            dma((bands,)),
        ],
        compiler_params=pltpu.CompilerParams(
            collective_id=0, has_side_effects=True, vmem_limit_bytes=58 << 20
        ),
    )(orient_index, spectra, bank, *tables)
    out = jax.ShapeDtypeStruct((2, 1, band, WCOLS), f32)
    one_mic = pl.BlockSpec((1, 1, band, WCOLS), lambda m: (m, 0, 0, 0))
    return pl.pallas_call(
        assemble_kernel,
        grid=(2,),
        out_shape=(out, out),
        in_specs=[pl.BlockSpec((2, band, WCOLS), lambda m: (m, 0, 0))],
        out_specs=(one_mic, one_mic),
    )(maps)


def shards(spectra, bank, orient_index):
    fits = (
        lax.axis_size("row") == 4
        and lax.axis_size("orient") == 2
        and spectra.shape[0] == 2
        and spectra.shape[2] == 4 * WCOLS
        and bank.shape[1] == 3 * WCOLS
        and spectra.shape[3] == 4 * spectra.shape[2]
    )
    body = shards_fused if fits else shards_general
    return body(spectra, bank, orient_index)


def solution(mesh):
    return jax.shard_map(
        shards,
        mesh=mesh,
        in_specs=(P(("grp", "mic"), None, "row", None), P(), P("grp")),
        out_specs=(P(("grp", "mic"), "row", None, None), P(("grp", "mic"), "row", None, None)),
        check_vma=False,
    )
```

```python
import functools
import math

import jax
import jax.numpy as jnp
import numpy as np
from jax import lax
from jax.experimental import pallas as pl
from jax.experimental.pallas import tpu as pltpu
from jax.sharding import PartitionSpec as P

WCOLS = 128
MESH = pl.DeviceIdType.MESH
EXTRA = 16
MAPS = jnp.bfloat16
CHUNKS = (64, 128, 128, 128, 64)
ORDER = (2, 3, 1, 0)


two_pi = 2.0 * math.pi


def swapped(shard, axis, apart):
    return lax.ppermute(shard, axis, [(i, i ^ 1 << apart) for i in range(lax.axis_size(axis))])


def merged_2(part, axis, combine):
    gathered = jax.tree.map(lambda a: lax.all_gather(a, axis), part)

    def take(source):
        return jax.tree.map(lambda a: lax.dynamic_index_in_dim(a, source, 0, False), gathered)

    return lax.fori_loop(
        1, lax.axis_size(axis), lambda source, state: combine(state, take(source)), take(0)
    )


def phase_table(row_start, row_count, col_start, col_count, period):
    row_ids = row_start + jnp.arange(row_count, dtype=jnp.int32)
    col_ids = col_start + jnp.arange(col_count, dtype=jnp.int32)
    wrapped = row_ids[:, None] * col_ids[None, :] % period
    angles = wrapped.astype(jnp.float32) * (two_pi / period)
    return (jnp.cos(angles), jnp.sin(angles))


def normalize(picture):
    values = picture.astype(jnp.float32)
    centred = values - jnp.mean(values)
    factor = lax.rsqrt(jnp.mean(centred * centred) + 1e-06)
    return (centred * factor).astype(jnp.bfloat16)


def reverse_bits(number, digits):
    result = number * 0
    for digit in range(digits):
        result = result + number // (1 << digit) % 2 * (1 << digits - 1 - digit)
    return result


def combine_maps(first_pair, second_pair):
    return (jnp.maximum(first_pair[0], second_pair[0]), first_pair[1] + second_pair[1])


def shards_general(spectra, bank, orient_index):
    mic_count = spectra.shape[0]
    band_rows = spectra.shape[2]
    length = spectra.shape[3]
    tsize_px = bank.shape[1]
    row_devices = lax.axis_size("row")
    row_place = lax.axis_index("row")
    share_count = orient_index.shape[0] // lax.axis_size("orient")
    chosen = lax.dynamic_slice_in_dim(
        orient_index, lax.axis_index("orient") * share_count, share_count
    )
    templates = jnp.stack(
        [
            normalize(lax.dynamic_index_in_dim(bank, chosen[place], 0, False))
            for place in range(share_count)
        ]
    )
    cos_y, sin_y = phase_table(row_place * band_rows, band_rows, 0, tsize_px, length)
    left_table = jnp.concatenate([cos_y.astype(jnp.bfloat16), -sin_y.astype(jnp.bfloat16)], 0)
    rowpass = jnp.einsum(
        "ay,oyx->oax", left_table, templates, preferred_element_type=jnp.float32
    ).astype(jnp.bfloat16)
    cos_x, sin_x = phase_table(0, tsize_px, 0, length, length)
    right_table = jnp.concatenate([cos_x.astype(jnp.bfloat16), sin_x.astype(jnp.bfloat16)], 1)
    mixed = jnp.einsum("oax,xk->oak", rowpass, right_table, preferred_element_type=jnp.float32)
    upper_rows = mixed[:, :band_rows]
    lower_rows = mixed[:, band_rows:]
    spec_re = upper_rows[:, :, :length] + lower_rows[:, :, length:]
    spec_im = lower_rows[:, :, :length] - upper_rows[:, :, length:]
    piece = jnp.stack([spec_re, spec_im], 1).astype(jnp.bfloat16)
    cos_e, sin_e = phase_table(0, length, 0, WCOLS, length)
    row_table = jnp.concatenate([cos_e.astype(jnp.bfloat16), sin_e.astype(jnp.bfloat16)], 1)
    updates = []
    for orient_pos in range(share_count):
        tmpl_re = piece[orient_pos, 0].astype(jnp.float32)
        tmpl_im = piece[orient_pos, 1].astype(jnp.float32)
        mic_re = spectra[:, 0].astype(jnp.float32)
        mic_im = spectra[:, 1].astype(jnp.float32)
        prod_re = mic_re * tmpl_re + mic_im * tmpl_im
        prod_im = mic_im * tmpl_re - mic_re * tmpl_im
        product = jnp.stack([prod_re, prod_im], 1).astype(jnp.bfloat16)
        summed = jnp.einsum("mcbk,kw->mcbw", product, row_table, preferred_element_type=jnp.float32)
        part_re = summed[:, 0, :, :WCOLS] - summed[:, 1, :, WCOLS:]
        part_im = summed[:, 0, :, WCOLS:] + summed[:, 1, :, :WCOLS]
        updates.append(jnp.stack([part_re, part_im], 1))
    partial_value = jnp.stack(updates, 1)
    item_total = mic_count * share_count
    values = partial_value.reshape(item_total, 2, band_rows, WCOLS)
    sections = row_devices.bit_length() - 1
    for bit in reversed(range(sections)):
        half_span = 1 << bit
        partner = swapped(values, "row", bit)
        upper_side = row_place // half_span % 2
        offset = row_place % half_span
        twist = offset.astype(jnp.float32) * (math.pi / half_span)
        twist_re = jnp.cos(twist)
        twist_im = jnp.sin(twist)
        differ = partner - values
        rot_re = differ[:, 0] * twist_re - differ[:, 1] * twist_im
        rot_im = differ[:, 0] * twist_im + differ[:, 1] * twist_re
        rotated = jnp.stack([rot_re, rot_im], 1)
        values = jnp.where(upper_side == 1, rotated, values + partner)
    residue = reverse_bits(row_place, sections)
    pixel_rows = residue + row_devices * jnp.arange(band_rows, dtype=jnp.int32)
    local_rows = jnp.arange(band_rows, dtype=jnp.int32)
    wrapped_col = pixel_rows[:, None] * local_rows[None, :] % length
    col_angles = wrapped_col.astype(jnp.float32) * (two_pi / length)
    column_table = jnp.stack([jnp.cos(col_angles), -jnp.sin(col_angles)], 1)
    corr = jnp.einsum("tcj,icjw->itw", column_table, values, precision=lax.Precision.HIGHEST)
    corr = corr * (1.0 / (length * tsize_px))
    corr = corr.reshape(mic_count, share_count, band_rows, WCOLS)
    peak_part = jnp.max(corr, axis=1)
    power_part = jnp.sum(corr * corr, axis=1)
    merged = merged_2((peak_part, power_part), "orient", combine_maps)
    return (merged[0][:, None], merged[1][:, None])


def rotation(rows, cols, period):
    angle = np.outer(rows, cols) % period * (two_pi / period)
    return np.cos(angle), np.sin(angle)


def fused_kernel(
    sizes,
    index_hbm, spectra_ref, bank_ref,
    enter_hbm, left_hbm, wide_hbm, short_hbm, leave_hbm, column_hbm, twc_hbm, tws_hbm,
    final,
    index, spec, bank, enter, left, wide, short, leave, column, twc, tws,
    template, own_s, send_s, recv_s, folded, rowpass, tspec, window, prod, p_send, p_all,
    v_all, corr_acc,
    own, sibling, merged,
    spec_sem, load_sem, fold_send, fold_recv, share_send, share_recv, send_sem, recv_sem,
    pair_send, pair_recv, map_send, map_recv, fwd_send, fwd_recv,
):
    bands, share, band, length, tsize = sizes
    half = WCOLS // 2
    hb = band // 2
    full = band + EXTRA
    win = tsize + WCOLS
    hw = win // 2
    me = lax.axis_index("row")
    core = lax.axis_index("orient")
    side = me // 2
    mirror = bands - 1 - me
    level = me + side * (mirror - me)
    peer = me + 1 - 2 * (me % 2)
    starts = [sum(CHUNKS[:k]) for k in range(len(CHUNKS))]
    count = len(CHUNKS)

    def spec_load(mic, k):
        start, n = starts[k], CHUNKS[k]
        row = start + side * (band - 2 * start - n)
        which = (1 - side) if mic == 0 else side
        return pltpu.make_async_copy(
            spectra_ref.at[which, :, pl.ds(pl.multiple_of(row, 16), n), :],
            spec.at[mic, :, pl.ds(start, n), :],
            spec_sem.at[mic, k],
        )

    first_rows = pl.ds(pl.multiple_of(level * band, band), full)
    loads = [
        pltpu.make_async_copy(source, target, load_sem.at[n])
        for n, (source, target) in enumerate(
            [
                (enter_hbm.at[core], enter),
                (bank_ref, bank),
                (left_hbm.at[:, first_rows, :], left),
                (short_hbm, short),
                (wide_hbm, wide),
                (leave_hbm.at[me % 2], leave),
                (column_hbm, column),
                (twc_hbm, twc),
                (tws_hbm, tws),
                (index_hbm, index),
            ]
        )
    ]
    spec_load(0, 0).start()
    loads[0].start()
    for k in range(1, count):
        spec_load(0, k).start()
    for k in range(count):
        spec_load(1, k).start()
    for load in loads[1:]:
        load.start()
    barrier = pltpu.get_barrier_semaphore()
    for k in range(1, bands):
        pl.semaphore_signal(
            barrier, inc=1, device_id={"row": lax.rem(me + k, bands)}, device_id_type=MESH
        )
    pl.semaphore_signal(barrier, inc=1, device_id={"orient": 1 - core}, device_id_type=MESH)

    flip = 1.0 - 2.0 * side.astype(jnp.float32)
    parity = (1 - 2 * core).astype(jnp.bfloat16)

    def chunk_rows(k):
        return pl.ds(starts[k], CHUNKS[k] + (EXTRA if k == count - 1 else 0))

    def fold_copy(k):
        rows = chunk_rows(k)
        return pltpu.make_async_remote_copy(
            src_ref=send_s.at[:, rows, :], dst_ref=recv_s.at[:, rows, :],
            send_sem=fold_send.at[k], recv_sem=fold_recv.at[k],
            device_id={"row": mirror}, device_id_type=MESH,
        )

    def enter_window(mic, target_ref, ks, carry):
        for k in ks:
            start, n = starts[k], CHUNKS[k]
            spec_load(mic, k).wait()
            if mic == 0 and k == 0:
                loads[0].wait()
            low = spec[mic, :, pl.ds(start, n), pl.ds(0, length // 2)]
            high = spec[mic, :, pl.ds(start, n), pl.ds(length // 2, length // 2)]
            mixed = (low + high * parity).reshape(2 * n, length // 2)
            value = jnp.dot(mixed, enter[...], preferred_element_type=jnp.float32)
            real = value[:n, :hw] - value[n:, hw:]
            imag = (value[:n, hw:] + value[n:, :hw]) * flip
            total = jnp.concatenate([real, imag], 1).astype(jnp.bfloat16)
            row_i = lax.broadcasted_iota(jnp.int32, (n, n), 0)
            col_i = lax.broadcasted_iota(jnp.int32, (n, n), 1)
            wanted = row_i + side * ((n - row_i) % n - row_i)
            turn = jnp.where(col_i == wanted, 1.0, 0.0).astype(jnp.bfloat16)
            turned = jnp.dot(turn, total, preferred_element_type=jnp.float32)
            rowid = lax.broadcasted_iota(jnp.int32, (n, win), 0)
            placed = jnp.where(rowid == side - 1, carry, turned).astype(jnp.bfloat16)
            carry = turned[0:1, :]
            for part in range(2):
                target_ref[part, pl.ds(start, n), :] = placed[:, part * hw : (part + 1) * hw]
            if k == count - 1:
                rowid = lax.broadcasted_iota(jnp.int32, (EXTRA, win), 0)
                last = jnp.where(rowid == side - 1, carry, 0.0).astype(jnp.bfloat16)
                for part in range(2):
                    target_ref[part, pl.ds(band, EXTRA), :] = last[:, part * hw : (part + 1) * hw]
            if mic == 0:
                send_chunk(k)
        return carry

    def send_chunk(k):
        if k == 0:
            pl.semaphore_wait(barrier, bands)
        fold_copy(k).start()

    blank = jnp.zeros((1, win), jnp.float32)
    enter_window(0, send_s, range(count), blank)

    for n in (1, 2, 3, 9):
        loads[n].wait()
    for o in range(share):
        picture = bank[index[core * share + o]].astype(jnp.float32)
        centred = picture - jnp.mean(picture)
        scale = lax.rsqrt(jnp.mean(centred * centred) + 1e-06)
        template[:, pl.ds(o * tsize, tsize)] = (centred * scale).astype(jnp.bfloat16)
    for part in range(2):
        for o in range(0, share, 2):
            cols = pl.ds(o * tsize, 2 * tsize)
            value = jnp.dot(left[part], template[:, cols], preferred_element_type=jnp.float32)
            rowpass[part, :, cols] = value.astype(jnp.bfloat16)
    for o in range(share):
        cols = pl.ds(o * tsize, tsize)
        for block in range(3):
            step = full // 3
            rows = pl.ds(block * step, step)
            re = jnp.dot(rowpass[0, rows, cols], short[...], preferred_element_type=jnp.float32)
            im = jnp.dot(rowpass[1, rows, cols], short[...], preferred_element_type=jnp.float32)
            tspec[o, rows, pl.ds(0, hw)] = re[:, :hw] + im[:, hw:]
            tspec[o, rows, pl.ds(hw, hw)] = re[:, :hw] - im[:, hw:]
            tspec[o, rows, pl.ds(win, hw)] = im[:, :hw] - re[:, hw:]
            tspec[o, rows, pl.ds(win + hw, hw)] = im[:, :hw] + re[:, hw:]
    for n in range(4, 9):
        loads[n].wait()

    def share_copy(k, source):
        rows = chunk_rows(k)
        return pltpu.make_async_remote_copy(
            src_ref=folded.at[source, :, rows, :], dst_ref=folded.at[source, :, rows, :],
            send_sem=share_send.at[k], recv_sem=share_recv.at[k],
            device_id={"orient": 1 - core}, device_id_type=MESH,
        )

    def part_copy(source, k):
        rows = chunk_rows(k)
        return pltpu.make_async_remote_copy(
            src_ref=p_send.at[:, rows, :], dst_ref=p_all.at[source, :, rows, :],
            send_sem=send_sem.at[k], recv_sem=recv_sem.at[k],
            device_id={"row": peer}, device_id_type=MESH,
        )

    def fold_chunk(k):
        rows = chunk_rows(k)
        fold_copy(k).wait_recv()
        total = own_s[:, rows, :].astype(jnp.float32) + recv_s[:, rows, :].astype(jnp.float32)
        folded[core, :, rows, :] = total.astype(jnp.bfloat16)
        share_copy(k, core).start()

    def product_chunk(k):
        rows = chunk_rows(k)
        n = CHUNKS[k] + (EXTRA if k == count - 1 else 0)
        share_copy(k, 1 - core).wait_recv()
        value = jnp.dot(
            folded[0, :, rows, :].reshape(2 * n, hw), wide[0], preferred_element_type=jnp.float32
        )
        value += jnp.dot(
            folded[1, :, rows, :].reshape(2 * n, hw), wide[1], preferred_element_type=jnp.float32
        )
        re, im = value[:n], value[n:]
        here = pl.ds(0, n)
        window[here, pl.ds(0, hw)] = re[:, :hw] + im[:, hw:]
        window[here, pl.ds(hw, hw)] = re[:, :hw] - im[:, hw:]
        window[here, pl.ds(win, hw)] = im[:, :hw] - re[:, hw:]
        window[here, pl.ds(win + hw, hw)] = im[:, :hw] + re[:, hw:]
        for o in range(share):
            there = pl.ds(o * n, n)
            m_re, m_im = window[here, pl.ds(0, win)], window[here, pl.ds(win, win)]
            t_re, t_im = tspec[o, rows, pl.ds(0, win)], tspec[o, rows, pl.ds(win, win)]
            prod[there, pl.ds(0, win)] = (m_re * t_re + m_im * t_im).astype(jnp.bfloat16)
            prod[there, pl.ds(win, win)] = (m_im * t_re - m_re * t_im).astype(jnp.bfloat16)
        value = jnp.dot(
            prod[pl.ds(0, share * n), :], leave[...], preferred_element_type=jnp.float32
        )
        value = value.astype(jnp.bfloat16)
        for o in range(share):
            p_send[o, rows, :] = value[o * n : (o + 1) * n, WCOLS:]
        part_copy(level, k).start()
        for o in range(share):
            p_all[level, o, rows, :] = value[o * n : (o + 1) * n, :WCOLS]

    factor = 1.0 / (length * tsize * win)

    def column_chunk(k):
        start, n = starts[k], CHUNKS[k]
        rows = pl.ds(start, n)
        part_copy(1 - level, k).wait_recv()
        for o in range(share):
            first = lax.broadcasted_iota(jnp.int32, (n, WCOLS), 1) < half
            b0, b1 = [p_all[b, o, rows, :].astype(jnp.float32) for b in range(2)]
            turned = pltpu.roll(b1, half, 1)
            turned = jnp.where(first, -turned, turned)
            u = [b0 + b1, b0 + turned, b0 - b1, b0 - turned]
            v = [u[0]]
            for rho in range(1, 4):
                span = pl.ds((rho - 1) * WCOLS, WCOLS)
                v.append(u[rho] * twc[rows, span] + pltpu.roll(u[rho], half, 1) * tws[rows, span])
            for pair in range(2):
                even, odd = v[2 * pair], v[2 * pair + 1]
                v_re = jnp.where(first, even, pltpu.roll(odd, half, 1))
                v_im = jnp.where(first, pltpu.roll(even, half, 1), odd)
                span = pl.ds((2 * o + pair) * WCOLS, WCOLS)
                for part, value in enumerate((v_re, v_im)):
                    high = value.astype(jnp.bfloat16)
                    v_all[pl.ds(part * n, n), span] = high
                    v_all[pl.ds((2 + part) * n, n), span] = high
                    v_all[pl.ds((4 + part) * n, n), span] = (
                        value - high.astype(jnp.float32)
                    ).astype(jnp.bfloat16)
        table = column[:, pl.ds(6 * start, 6 * n)]
        corr = jnp.dot(table, v_all[pl.ds(0, 6 * n), :], preferred_element_type=jnp.float32)
        if k == 0:
            corr_acc[...] = corr
        else:
            corr_acc[...] += corr

    carried = blank
    for k in range(count):
        carried = enter_window(1, own_s, (k,), carried)
        fold_chunk(k)
        if k > 1:
            column_chunk(k - 2)
        product_chunk(k)
    column_chunk(count - 2)
    column_chunk(count - 1)

    edge = []
    for o in range(share):
        e0, e1 = [p_all[b, o, pl.ds(band, EXTRA), :].astype(jnp.float32) for b in range(2)]
        first = lax.broadcasted_iota(jnp.int32, (EXTRA, WCOLS), 1) < half
        swapped_0, swapped_1 = pltpu.roll(e0, half, 1), pltpu.roll(e1, half, 1)
        edge.append(
            [
                jnp.where(first, e0 + e1, -e0 - swapped_1)[0:1, :],
                jnp.where(first, e1 - e0, e0 - swapped_1)[0:1, :],
            ]
        )

    first = lax.broadcasted_iota(jnp.int32, (band, WCOLS), 1) < half
    for pair in range(2):
        hi = po = None
        for o in range(share):
            corr = (corr_acc[:, pl.ds((2 * o + pair) * WCOLS, WCOLS)] + edge[o][pair]) * factor
            hi = corr if o == 0 else jnp.maximum(hi, corr)
            po = corr * corr if o == 0 else po + corr * corr
        own[pair] = jnp.where(first, hi, pltpu.roll(po, half, 1))
        own[pair + 2] = jnp.where(first, pltpu.roll(hi, half, 1), po)

    mine = pl.ds(pl.multiple_of(core * hb, hb), hb)
    theirs = pl.ds(pl.multiple_of((1 - core) * hb, hb), hb)

    def target_of(k):
        if k == 0:
            return me
        return peer if k == 1 else (1 - side) * 2 + (k - 2 + me) % 2

    def swap(k):
        q = target_of(k)
        return pltpu.make_async_remote_copy(
            src_ref=own.at[q, theirs, :], dst_ref=sibling.at[q],
            send_sem=pair_send.at[k], recv_sem=pair_recv.at[k],
            device_id={"orient": 1 - core}, device_id_type=MESH,
        )

    for k in ORDER:
        swap(k).start()
    first = lax.broadcasted_iota(jnp.int32, (hb, WCOLS), 1) < half

    def map_copy(k, source):
        dest = target_of(k)
        return pltpu.make_async_remote_copy(
            src_ref=merged.at[dest], dst_ref=final.at[source, mine, :],
            send_sem=map_send.at[k], recv_sem=map_recv.at[source],
            device_id={"row": dest}, device_id_type=MESH,
        )

    def forward(source, rows):
        return pltpu.make_async_remote_copy(
            src_ref=final.at[source, rows, :], dst_ref=final.at[source, rows, :],
            send_sem=fwd_send.at[source], recv_sem=fwd_recv.at[source],
            device_id={"orient": 1 - core}, device_id_type=MESH,
        )

    for k in ORDER:
        swap(k).wait_recv()
        q = target_of(k)
        one, two = own[q, mine, :], sibling[q]
        total = jnp.where(first, jnp.maximum(one, two), one + two).astype(final.dtype)
        if k == 0:
            final[me, mine, :] = total
        else:
            merged[q] = total
            map_copy(k, me).start()
    forward(me, mine).start()
    for k in (1, 2, 3):
        source = target_of(k)
        map_copy(k, source).wait_recv()
        forward(source, mine).start()
    for source in range(4):
        forward(source, theirs).wait_recv()
    for source in range(4):
        forward(source, mine).wait_send()
    for k in range(1, bands):
        map_copy(k, me).wait_send()
    for k in range(bands):
        swap(k).wait_send()
    for k in range(count):
        fold_copy(k).wait_send()
        share_copy(k, core).wait_send()
        part_copy(level, k).wait_send()


def assemble_kernel(maps, peak_ref, power_ref):
    half = WCOLS // 2
    first = lax.broadcasted_iota(jnp.int32, maps.shape[1:], 1) < half
    a, b = maps[0].astype(jnp.float32), maps[1].astype(jnp.float32)
    peak_ref[0, 0] = jnp.where(first, a, pltpu.roll(b, half, 1))
    power_ref[0, 0] = jnp.where(first, pltpu.roll(a, half, 1), b)


def shards_fused(spectra, bank, orient_index):
    band = spectra.shape[2]
    length = spectra.shape[3]
    tsize = bank.shape[1]
    bands = lax.axis_size("row")
    share = orient_index.shape[0] // lax.axis_size("orient")
    half = WCOLS // 2
    win = tsize + WCOLS
    hw = win // 2
    count = len(CHUNKS)
    full = band + EXTRA
    bf, f32 = jnp.bfloat16, jnp.float32

    def low(table):
        return np.ascontiguousarray(table).astype(np.float32).astype(bf)

    def blocks(re, im):
        return np.concatenate([np.concatenate([re, im], 1), np.concatenate([-im, re], 1)], 0)

    kx = np.arange(length // 2)
    place = np.arange(hw)
    enter = np.stack([np.concatenate(rotation(kx, 2 * place + c, length), 1) for c in range(2)])
    ky = np.arange(2 * band + EXTRA)
    cos_y, sin_y = rotation(ky, np.arange(tsize), length)
    left = np.stack([cos_y, -sin_y])
    freq = np.arange(hw) + 0.5
    wide = np.stack([np.concatenate(rotation(2 * place + c, freq, win), 1) for c in range(2)])
    short = np.concatenate(rotation(np.arange(tsize), freq, win), 1)
    both = np.concatenate([freq, -freq])
    leave = []
    for xh in range(2):
        tiles = []
        for h in (xh, 1 - xh):
            tiles.append(blocks(*rotation(both, h * half + np.arange(half), win)))
        leave.append(np.concatenate(tiles, 1))
    leave = np.stack(leave)
    column = []
    for k, n in enumerate(CHUNKS):
        col_j = sum(CHUNKS[:k]) + np.arange(n)
        cos_c, sin_c = rotation(np.arange(band), col_j, band)
        exact = np.concatenate([cos_c, -sin_c], 1).astype(np.float32)
        high = low(exact).astype(np.float32)
        column += [high, exact - high, high]
    column = np.concatenate(column, 1)
    rho = np.repeat(np.arange(1, 4), WCOLS)
    twc, tws = rotation(np.arange(band), rho, length)
    tws = np.where(np.arange(3 * WCOLS) % WCOLS < half, -tws, tws)
    tables = [
        low(enter), low(left), low(wide), low(short), low(leave), low(column),
        twc.astype(np.float32), tws.astype(np.float32),
    ]
    vmem = pl.BlockSpec(memory_space=pltpu.VMEM)
    hbm = pl.BlockSpec(memory_space=pl.ANY)
    dma = pltpu.SemaphoreType.DMA
    maps = pl.pallas_call(
        functools.partial(fused_kernel, (bands, share, band, length, tsize)),
        out_shape=jax.ShapeDtypeStruct((4, band, WCOLS), MAPS),
        in_specs=[hbm] * (3 + len(tables)),
        out_specs=vmem,
        scratch_shapes=[
            pltpu.SMEM(orient_index.shape, jnp.int32),
            pltpu.VMEM(spectra.shape, bf),
            pltpu.VMEM(bank.shape, bf),
            pltpu.VMEM((length // 2, win), bf),
            pltpu.VMEM((2, full, tsize), bf),
            pltpu.VMEM((2, hw, win), bf),
            pltpu.VMEM((tsize, win), bf),
            pltpu.VMEM((2 * win, 2 * WCOLS), bf),
            pltpu.VMEM((band, 6 * band), bf),
            pltpu.VMEM((band, 3 * WCOLS), f32),
            pltpu.VMEM((band, 3 * WCOLS), f32),
            pltpu.VMEM((tsize, share * tsize), bf),
            pltpu.VMEM((2, full, hw), bf),
            pltpu.VMEM((2, full, hw), bf),
            pltpu.VMEM((2, full, hw), bf),
            pltpu.VMEM((2, 2, full, hw), bf),
            pltpu.VMEM((2, full, share * tsize), bf),
            pltpu.VMEM((share, full, 2 * win), f32),
            pltpu.VMEM((max(CHUNKS) + EXTRA, 2 * win), f32),
            pltpu.VMEM((share * (max(CHUNKS) + EXTRA), 2 * win), bf),
            pltpu.VMEM((share, full, WCOLS), bf),
            pltpu.VMEM((2, share, full, WCOLS), bf),
            pltpu.VMEM((6 * max(CHUNKS), 2 * share * WCOLS), bf),
            pltpu.VMEM((band, 2 * share * WCOLS), f32),
            pltpu.VMEM((4, band, WCOLS), f32),
            pltpu.VMEM((4, band // 2, WCOLS), f32),
            pltpu.VMEM((4, band // 2, WCOLS), MAPS),
            dma((2, count)),
            dma((10,)),
            dma((count,)),
            dma((count,)),
            dma((count,)),
            dma((count,)),
            dma((count,)),
            dma((count,)),
            dma((bands,)),
            dma((bands,)),
            dma((bands,)),
            dma((bands,)),
            dma((bands,)),
            dma((bands,)),
        ],
        compiler_params=pltpu.CompilerParams(
            collective_id=0, has_side_effects=True, vmem_limit_bytes=58 << 20
        ),
    )(orient_index, spectra, bank, *tables)
    out = jax.ShapeDtypeStruct((2, 1, band, WCOLS), f32)
    one_mic = pl.BlockSpec((1, 1, band, WCOLS), lambda m: (m, 0, 0, 0))
    return pl.pallas_call(
        assemble_kernel,
        grid=(2,),
        out_shape=(out, out),
        in_specs=[pl.BlockSpec((2, band, WCOLS), lambda m: (m, 0, 0))],
        out_specs=(one_mic, one_mic),
    )(maps)


def shards(spectra, bank, orient_index):
    fits = (
        lax.axis_size("row") == 4
        and lax.axis_size("orient") == 2
        and spectra.shape[0] == 2
        and spectra.shape[2] == 4 * WCOLS
        and bank.shape[1] == 3 * WCOLS
        and spectra.shape[3] == 4 * spectra.shape[2]
    )
    body = shards_fused if fits else shards_general
    return body(spectra, bank, orient_index)


def solution(mesh):
    return jax.shard_map(
        shards,
        mesh=mesh,
        in_specs=(P(("grp", "mic"), None, "row", None), P(), P("grp")),
        out_specs=(P(("grp", "mic"), "row", None, None), P(("grp", "mic"), "row", None, None)),
        check_vma=False,
    )
```
